32 devices in a mesh: tm: 8 (over z, y), head: 4 (over x, core).
Axes of the slice: x: 2, y: 2, z: 4, core: 2. Of those that a mesh axis runs over, the one named last changes fastest.
Arguments:
- queries: bfloat16 [2048, 3072], P('tm', 'head'), may hold values from -6 to 6
- key_input: bfloat16 [2048, 3072], P('tm', 'head'), may hold values from -6 to 6
- values: bfloat16 [2048, 3072], P('tm', 'head'), may hold values from -6 to 6
- query_gain: float32 [128], replicated, may hold values from 0.25 to 1.75
- key_gain: float32 [128], replicated, may hold values from 0.25 to 1.75
- frames: int32 [4], replicated, may hold values from 1 to 8, 16 in all
- frame_rate: int32 [4], replicated, may hold values from 8 to 30
- out_weight: bfloat16 [24, 3072, 128], P('head', 'tm'), may hold values from -0.109375 to 0.109375
Outputs:
- mixed: bfloat16 [2048, 3072], P('tm', 'head')
The draws below stay inside these ranges and needn't reach their ends.
Inputs may be any that keep to these rules, and one draw needn't show every extreme that they name: The clips' frames, in order, make up all 16 frames; the longest clip has exactly 8 frames.
All inputs are finite; a program needn't handle non-finite values.
Results may differ from the reference program's by a relative error of at most 0.0084.
Values may be sent and summed in bfloat16 or wider, within the bound.
A program may use at most 64 MiB of HBM per device.

```python
import math
import jax
import jax.numpy as jnp
import numpy as np
from jax import lax

D = 3072
H = 24
HD = 128
GW = 16
WIN = 12
NCLIPS = 4
SPAN = 7
FRAME = 128
TOK_DEV = 256
FRAMES = 16
TOKENS = 2048
MAXF = 8


def set_ends(result, key, smallest, largest):
    index_at = [jax.random.randint(jax.random.fold_in(key, axis), (), 0, length) for axis, length in enumerate(result.shape)]
    main_axis = result.shape.index(max(result.shape))
    neighbour = index_at[:main_axis] + [(index_at[main_axis] + 1) % result.shape[main_axis]] + index_at[main_axis + 1:]
    return result.at[tuple(index_at)].set(smallest).at[tuple(neighbour)].set(largest)


def steps_of(key, shape, split, low, largest):
    loudness, own = 1.0, jax.random.fold_in(key, 6)
    for position, shards_of in split:
        steps = jnp.exp(jax.random.uniform(jax.random.fold_in(own, position), (shards_of,), jnp.float32, low / len(split), largest / len(split)))
        loudness = loudness * jnp.repeat(steps, shape[position] // shards_of).reshape([-1 if axis == position else 1 for axis in range(len(shape))])
    return loudness


def profile(number_of, total, most, lean):
    weights = [(1 << 20) // math.isqrt(standing ** lean) + 1 for standing in range(2, number_of + 1)]
    rest, given = total - most - (number_of - 1), [1] * (number_of - 1)
    while rest > 0:
        movable = [i for i in range(number_of - 1) if given[i] < most]
        mass, budget = sum([weights[i] for i in movable]), rest
        for i in movable:
            more = min(most - given[i], max(1, budget * weights[i] // mass), rest)
            given[i] = given[i] + more
            rest = rest - more
    return np.array([most] + given)


def ragged_sizes(rng, number_of, total, most, lean):
    if number_of == 2:
        one = jax.random.randint(rng, (), max(1, total - most), min(most, total - 1) + 1)
        return jnp.stack([one, total - one])
    tallies = jnp.asarray(profile(number_of, total, most, lean), jnp.int32)
    twos = (number_of - 1) // 2
    source_of, sink = tallies[1:1 + 2 * twos:2], tallies[2:2 + 2 * twos:2]
    margin = jnp.minimum(source_of - 1, most - sink)
    moved = jax.random.randint(jax.random.fold_in(rng, 1), (twos,), 0, 1 << 20) % (margin + 1)
    tallies = tallies.at[1:1 + 2 * twos:2].set(source_of - moved).at[2:2 + 2 * twos:2].set(sink + moved)
    return tallies[jax.random.permutation(jax.random.fold_in(rng, 2), number_of)]


def normal_values(own_key, shape, scale, bound, shards=(), held_as=jnp.bfloat16):
    loudness = steps_of(own_key, shape, shards, -0.22, 0.18) if shards else 1.0
    drawn = jax.random.normal(own_key, shape, jnp.float32) * scale * loudness
    return jnp.minimum(jnp.maximum(drawn, -bound), bound).astype(held_as)


def setup_inputs(seed: int = 0) -> dict:
    seeds = jax.random.split(jax.random.key(seed), 9)
    queries = normal_values(seeds[0], (TOKENS, H * HD), 1.0, 6.0, ((0, 8), (1, 4)))
    key_input = normal_values(seeds[1], (TOKENS, H * HD), 1.0, 6.0, ((0, 8), (1, 4)))
    values = normal_values(seeds[2], (TOKENS, H * HD), 1.0, 6.0, ((0, 8), (1, 4)))
    query_gain = jnp.clip(1.0 + 0.15 * jax.random.normal(seeds[3], (HD,), jnp.float32), 0.25, 1.75)
    key_gain = jnp.clip(1.0 + 0.15 * jax.random.normal(seeds[4], (HD,), jnp.float32), 0.25, 1.75)
    frames = ragged_sizes(seeds[5], NCLIPS, FRAMES, MAXF, 2).astype(jnp.int32)
    frame_rate = set_ends(jax.random.randint(seeds[6], (NCLIPS,), 8, 31), jax.random.fold_in(seeds[6], 1), 8, 30).astype(jnp.int32)
    out_weight = normal_values(seeds[7], (H, D, HD), (H * HD) ** -0.5, 0.109375, ((0, 4), (1, 8)))
    return dict(queries=queries, key_input=key_input, values=values, query_gain=query_gain, key_gain=key_gain, frames=frames, frame_rate=frame_rate, out_weight=out_weight)


def rope_freqs(width):
    steps = jnp.arange(width // 2, dtype=jnp.float32)
    return jnp.exp(steps * (-2.0 * math.log(10000.0) / width))

def clip_of(token_index, frames):
    ends = jnp.cumsum(frames).astype(jnp.int32)
    starts = (ends - frames).astype(jnp.int32)
    frame_global = (token_index // FRAME).astype(jnp.int32)
    inside = ((frame_global[:, None] >= starts[None, :]) & (frame_global[:, None] < ends[None, :])).astype(jnp.int32)
    clip_id = lax.optimization_barrier(jnp.sum(inside * jnp.arange(frames.shape[0], dtype=jnp.int32)[None, :], axis=1)).astype(jnp.int32)
    return (clip_id, frame_global, inside, starts)

def rotary(token_index, frames, frame_rate, head_size):
    clip_id, frame_global, inside, starts = clip_of(token_index, frames)
    frame_start = lax.optimization_barrier(jnp.sum(inside * starts[None, :], axis=1)).astype(jnp.int32)
    rate_token = lax.optimization_barrier(jnp.sum(inside * frame_rate[None, :], axis=1)).astype(jnp.float32)
    in_frame = token_index % FRAME
    time_pos = (frame_global - frame_start).astype(jnp.float32) * 24.0 / rate_token
    row_pos = (in_frame // GW).astype(jnp.float32)
    col_pos = (in_frame % GW).astype(jnp.float32)
    side = head_size // 6 * 2
    depth = head_size - 2 * side
    angles = jnp.concatenate([time_pos[:, None] * rope_freqs(depth)[None, :], row_pos[:, None] * rope_freqs(side)[None, :], col_pos[:, None] * rope_freqs(side)[None, :]], axis=1)
    return (clip_id, frame_global, jnp.cos(angles), jnp.sin(angles))

def norm_rotate(rows, gain, cosine, sine):
    values_f = rows.astype(jnp.float32)
    mean_sq = lax.optimization_barrier(jnp.mean(values_f * values_f, axis=-1, keepdims=True))
    normed = values_f * lax.rsqrt(mean_sq + 1e-06) * gain
    half = rows.shape[-1] // 2
    first, second = (normed[..., :half], normed[..., half:])
    cos_b = cosine[:, None, :]
    sin_b = sine[:, None, :]
    return jnp.concatenate([first * cos_b - second * sin_b, second * cos_b + first * sin_b], axis=-1).astype(jnp.bfloat16)

def reference(queries, key_input, values, query_gain, key_gain, frames, frame_rate, out_weight):
    total = queries.shape[0]
    head_count = H
    head_size = HD
    block_rows = TOK_DEV
    index_all = jnp.arange(total, dtype=jnp.int32)
    clip_all, frame_all, cos_all, sin_all = rotary(index_all, frames, frame_rate, head_size)
    q_rot = norm_rotate(queries.reshape(total, head_count, head_size), query_gain, cos_all, sin_all)
    k_rot = norm_rotate(key_input.reshape(total, head_count, head_size), key_gain, cos_all, sin_all)
    v_rows = values.reshape(total, head_count, head_size)
    back = (SPAN - 1) * block_rows
    k_pad = jnp.concatenate([jnp.zeros((back, head_count, head_size), jnp.bfloat16), k_rot], axis=0)
    v_pad = jnp.concatenate([jnp.zeros((back, head_count, head_size), jnp.bfloat16), v_rows], axis=0)
    clip_pad = jnp.concatenate([jnp.full((back,), -1, jnp.int32), clip_all], axis=0)
    frame_pad = jnp.concatenate([jnp.zeros((back,), jnp.int32), frame_all], axis=0)
    w_mat = jnp.transpose(out_weight, (0, 2, 1)).reshape(head_count * head_size, out_weight.shape[1])

    def one_block(block_id):
        first_row = (block_id * block_rows).astype(jnp.int32)
        q_block = lax.dynamic_slice_in_dim(q_rot, first_row, block_rows, 0)
        q_clip = lax.dynamic_slice_in_dim(clip_all, first_row, block_rows, 0)
        q_frame = lax.dynamic_slice_in_dim(frame_all, first_row, block_rows, 0)
        k_block = lax.dynamic_slice_in_dim(k_pad, first_row, SPAN * block_rows, 0)
        v_block = lax.dynamic_slice_in_dim(v_pad, first_row, SPAN * block_rows, 0)
        k_clip = lax.dynamic_slice_in_dim(clip_pad, first_row, SPAN * block_rows, 0)
        k_frame = lax.dynamic_slice_in_dim(frame_pad, first_row, SPAN * block_rows, 0)
        key_mask = (k_clip[None, :] == q_clip[:, None]) & (k_frame[None, :] <= q_frame[:, None]) & (k_frame[None, :] >= q_frame[:, None] - (WIN - 1))
        scores = jnp.einsum('qhe,khe->hqk', q_block.astype(jnp.float32), k_block.astype(jnp.float32)) / math.sqrt(head_size)
        probs = jnp.where(key_mask[None, :, :], jnp.exp(scores), 0.0)
        denom = lax.optimization_barrier(jnp.sum(probs, axis=2))
        probs_b = lax.optimization_barrier(probs.astype(jnp.bfloat16)).astype(jnp.float32)
        numerator = jnp.einsum('hqk,khe->qhe', probs_b, v_block.astype(jnp.float32))
        attended = (numerator / jnp.transpose(denom)[:, :, None]).astype(jnp.bfloat16)
        flat = attended.reshape(block_rows, head_count * head_size)
        return jnp.dot(flat, w_mat, preferred_element_type=jnp.float32).astype(jnp.bfloat16)
    blocks = lax.map(one_block, jnp.arange(total // block_rows, dtype=jnp.int32))
    return blocks.reshape(total, out_weight.shape[1])
```

```python
import functools
import math

import jax
import jax.numpy as jnp
from jax import lax
from jax.experimental import pallas as pl
from jax.experimental.pallas import tpu as pltpu
from jax.sharding import PartitionSpec as P

GW = 16
WIN = 12
FRAME = 128
MESH = pl.DeviceIdType.MESH


def rope_freqs(width):
    steps = jnp.arange(width // 2, dtype=jnp.float32)
    return jnp.exp(steps * (-2.0 * math.log(10000.0) / width))


def clip_of(frame_global, frames):
    ends = jnp.cumsum(frames)
    starts = ends - frames
    inside = (
        (frame_global[:, None] >= starts[None, :]) & (frame_global[:, None] < ends[None, :])
    ).astype(jnp.int32)
    clip_id = jnp.sum(inside * jnp.arange(frames.shape[0], dtype=jnp.int32)[None, :], axis=1)
    return (clip_id, inside, starts)


def rotary(token_index, frames, frame_rate, head_size):
    frame_global = token_index // FRAME
    clip_id, inside, starts = clip_of(frame_global, frames)
    frame_start = jnp.sum(inside * starts[None, :], axis=1)
    rate_token = jnp.sum(inside * frame_rate[None, :], axis=1).astype(jnp.float32)
    in_frame = token_index % FRAME
    time_pos = (frame_global - frame_start).astype(jnp.float32) * 24.0 / rate_token
    row_pos = (in_frame // GW).astype(jnp.float32)
    col_pos = (in_frame % GW).astype(jnp.float32)
    side = head_size // 6 * 2
    depth = head_size - 2 * side
    angles = jnp.concatenate(
        [
            time_pos[:, None] * rope_freqs(depth)[None, :],
            row_pos[:, None] * rope_freqs(side)[None, :],
            col_pos[:, None] * rope_freqs(side)[None, :],
        ],
        axis=1,
    )
    return (jnp.cos(angles), jnp.sin(angles))


def norm_rotate(rows, gain, cosine, sine):
    values_f = rows.astype(jnp.float32)
    mean_sq = jnp.mean(values_f * values_f, axis=-1, keepdims=True)
    normed = values_f * lax.rsqrt(mean_sq + 1e-06) * gain
    half = rows.shape[-1] // 2
    first, second = (normed[..., :half], normed[..., half:])
    cos_b = cosine[:, None, :]
    sin_b = sine[:, None, :]
    return jnp.concatenate(
        [first * cos_b - second * sin_b, second * cos_b + first * sin_b], axis=-1
    ).astype(jnp.bfloat16)


def kernel(cfg, q_ref, k_ref, v_ref, w_ref, mask_ref, out_ref,
           ka, va, kb, vb, wg, num, den, att, ptx, keep, rx1, stx, rx2, ytx, yrx,
           up_s, up_r, pt_s, pt_r, wu_s, wu_r, wd_s, wd_r, at_s, at_r,
           c_s, c_r, h_s, h_r, y_s, y_r, loc):
    n_out, reach, steps, q_cnt, heads, hs = cfg
    rows = q_ref.shape[0]
    pos = lax.axis_index("tm")
    head = lax.axis_index("head")
    o, b = pos // 2, pos % 2
    hi, lo = head // 2, head % 2
    partner = pos + 1 - 2 * b
    core = head + 1 - 2 * lo
    cross = lax.rem(head + 2, 4)
    has_up = o + 1 < n_out
    has_dn = o >= 1

    barrier = pltpu.get_barrier_semaphore()
    pl.semaphore_signal(barrier, inc=1, device_id={"tm": partner}, device_id_type=MESH)
    pl.semaphore_signal(barrier, inc=1, device_id={"head": core}, device_id_type=MESH)
    pl.semaphore_signal(barrier, inc=1, device_id={"head": cross}, device_id_type=MESH)

    @pl.when(has_up)
    def _():
        pl.semaphore_signal(barrier, inc=1, device_id={"tm": pos + 2}, device_id_type=MESH)

    @pl.when(has_dn)
    def _():
        pl.semaphore_signal(barrier, inc=1, device_id={"tm": pos - 2}, device_id_type=MESH)

    amount = 3 + has_up.astype(jnp.int32) + has_dn.astype(jnp.int32)
    pl.semaphore_wait(barrier, amount)

    def rcopy(src, dst, s, r, axis, index):
        return pltpu.make_async_remote_copy(
            src_ref=src, dst_ref=dst, send_sem=s, recv_sem=r,
            device_id={axis: index}, device_id_type=MESH)

    def a_ref(s):
        return (k_ref, v_ref) if s == 0 else (ka.at[s - 1], va.at[s - 1])

    def up_kv(s):
        src, dst = a_ref(s - 1), a_ref(s)
        return [rcopy(src[i], dst[i], up_s.at[s - 1, i], up_r.at[s - 1, i], "tm", pos + 2)
                for i in range(2)]

    def pair_kv(s):
        src, dst = a_ref(s), (kb.at[s], vb.at[s])
        return [rcopy(src[i], dst[i], pt_s.at[s, i], pt_r.at[s, i], "tm", partner)
                for i in range(2)]

    def needs(s):
        return (s >= 1 and 2 * s - 1 <= reach, 2 * s + 1 <= reach)

    def pair_gets(s):
        n0, n1 = needs(s)
        return (o >= s) & (((b == 0) & n0) | ((b == 1) & n1))

    def pair_sends(s):
        n0, n1 = needs(s)
        return (o >= s) & (((b == 1) & n0) | ((b == 0) & n1))

    def w_up(t):
        origin = jnp.maximum(o - t + 1, 0)
        return rcopy(wg.at[origin], wg.at[origin], wu_s.at[t - 1], wu_r.at[t - 1], "tm", pos + 2)

    def w_dn(t):
        origin = jnp.minimum(o + t - 1, n_out - 1)
        return rcopy(wg.at[origin], wg.at[origin], wd_s.at[t - 1], wd_r.at[t - 1], "tm", pos - 2)

    def start_all(cond, copies):
        @pl.when(cond)
        def _():
            for c in copies:
                c.start()

    def wait_recv(cond, copies):
        @pl.when(cond)
        def _():
            for c in copies:
                c.wait_recv()

    def wait_send(cond, copies):
        @pl.when(cond)
        def _():
            for c in copies:
                c.wait_send()

    def up_sends(t):
        return has_up & (o - t + 1 >= 0)

    def dn_sends(t):
        return has_dn & (o + t - 1 < n_out)

    scale = 1.0 / math.sqrt(hs)

    def attend(key_ref, value_ref, slot, first=False):
        mask = jnp.concatenate(
            [jnp.broadcast_to(mask_ref[slot, f:f + 1, :], (FRAME, rows))
             for f in range(rows // FRAME)], axis=0)

        def one(h, carry):
            at = pl.ds(pl.multiple_of(h * hs, hs), hs)
            scores = lax.dot_general(q_ref[:, at], key_ref[:, at], (((1,), (1,)), ((), ())),
                                     preferred_element_type=jnp.float32)
            probs = jnp.exp(scores * scale) * mask
            total = jnp.sum(probs, axis=1, keepdims=True)
            part = jnp.dot(probs.astype(jnp.bfloat16), value_ref[:, at],
                           preferred_element_type=jnp.float32)
            if first:
                den[h] = total
                num[:, at] = part
            else:
                den[h] += total
                num[:, at] += part
            return carry

        lax.fori_loop(0, heads, one, 0)

    start_all(has_up, up_kv(1))
    start_all(pair_sends(0), pair_kv(0))
    own = pltpu.make_async_copy(w_ref, wg.at[o], loc)
    own.start()
    own.wait()
    start_all(dn_sends(1), [w_dn(1)])
    attend(k_ref, v_ref, 0, first=True)

    def down(t):
        wait_recv(o + t < n_out, [w_dn(t)])
        if t + 1 < n_out:
            start_all(dn_sends(t + 1), [w_dn(t + 1)])

    def up(t):
        wait_recv(o - t >= 0, [w_up(t)])
        if t + 1 < n_out:
            start_all(up_sends(t + 1), [w_up(t + 1)])

    def use_pair(s):
        @pl.when(pair_gets(s))
        def _():
            for c in pair_kv(s):
                c.wait_recv()
            attend(kb.at[s], vb.at[s], steps + 1 + s)

    for s in range(1, steps + 1):
        if s < n_out:
            down(s)
        wait_recv(o >= s, up_kv(s))
        if s < steps:
            start_all(has_up & (o >= s), up_kv(s + 1))
        start_all(pair_sends(s), pair_kv(s))
        if s == max(steps - 1, 1):
            start_all(up_sends(1), [w_up(1)])
        if any(needs(s - 1)):
            use_pair(s - 1)
        if 2 * s <= reach:
            @pl.when(o >= s)
            def _():
                attend(*a_ref(s), s)
    for t in range(steps + 1, n_out):
        down(t)
    up(1)
    use_pair(steps)

    for h in range(heads):
        at = slice(h * hs, (h + 1) * hs)
        att[0:rows, at] = (num[:, at] / den[h]).astype(jnp.bfloat16)
    swap = rcopy(att.at[pl.ds(0, rows)], att.at[pl.ds(rows, rows)], at_s, at_r, "tm", partner)
    swap.start()
    for t in range(2, n_out):
        up(t)
    swap.wait_recv()

    def project(group, store):
        def one(k, carry):
            acc = None
            for h in range(heads):
                part = lax.dot_general(
                    att[:, h * hs:(h + 1) * hs], wg[group * q_cnt + k, h],
                    (((1,), (1,)), ((), ())), preferred_element_type=jnp.float32)
                acc = part if acc is None else acc + part
            store(k, acc)
            return carry
        if q_cnt == 1:
            one(0, 0)
        else:
            lax.fori_loop(0, q_cnt, one, 0)

    sides = (1 - hi, hi)
    c_copies = []
    for i, side in enumerate(sides):
        def put(k, acc, i=i):
            ptx[i, k] = acc.astype(jnp.bfloat16)
        project(2 * side + (1 - lo), put)
        copy = rcopy(ptx.at[i], rx1.at[i], c_s.at[i], c_r.at[i], "head", core)
        copy.start()
        c_copies.append(copy)
    for i, side in enumerate(sides):
        def put(k, acc, i=i):
            keep[i, k] = acc
        project(2 * side + lo, put)
    c_copies[0].wait_recv()
    h_copies = [None, None]
    for r in (1, 0):
        at = slice(r * rows, (r + 1) * rows)
        stx[r] = (keep[0, :, at] + rx1[0, :, at].astype(jnp.float32)).astype(jnp.bfloat16)
        h_copies[r] = rcopy(stx.at[r], rx2.at[r], h_s.at[r], h_r.at[r], "head", cross)
        h_copies[r].start()
    c_copies[1].wait_recv()

    def final(r):
        at = slice(r * rows, (r + 1) * rows)
        mine = keep[1, :, at] + rx1[1, :, at].astype(jnp.float32)
        return (mine + rx2[r].astype(jnp.float32)).astype(jnp.bfloat16)

    h_copies[1].wait_recv()
    ytx[...] = final(1)
    y_copy = rcopy(ytx, yrx, y_s, y_r, "tm", partner)
    y_copy.start()
    h_copies[0].wait_recv()
    out_ref[b] = final(0)
    y_copy.wait_recv()
    out_ref[1 - b] = yrx[...]

    for s in range(1, steps + 1):
        wait_send(has_up & (o >= s - 1), up_kv(s))
    for s in range(steps + 1):
        if any(needs(s)):
            wait_send(pair_sends(s), pair_kv(s))
    for t in range(1, n_out):
        wait_send(up_sends(t), [w_up(t)])
        wait_send(dn_sends(t), [w_dn(t)])
    for c in [swap, y_copy] + c_copies + h_copies:
        c.wait_send()


def per_device(queries, key_input, values, query_gain, key_gain, frames, frame_rate, out_weight):
    rows = queries.shape[0]
    hs = query_gain.shape[0]
    heads = queries.shape[1] // hs
    n = lax.axis_size("tm")
    m = lax.axis_size("head")
    n_out = n // 2
    per = rows // FRAME
    longest = n * per // 2
    back = min(WIN, longest) - 1
    reach = min((back + per - 1) // per, n - 1)
    steps = (reach + 1) // 2
    q_cnt = n_out // m
    dsl = out_weight.shape[1]

    pos = lax.axis_index("tm")
    b = pos % 2
    own_index = pos * rows + jnp.arange(rows, dtype=jnp.int32)
    cosine, sine = rotary(own_index, frames, frame_rate, hs)
    q_rot = norm_rotate(queries.reshape(rows, heads, hs), query_gain, cosine, sine)
    k_rot = norm_rotate(key_input.reshape(rows, heads, hs), key_gain, cosine, sine)

    back_by = jnp.stack([jnp.int32(2 * s) for s in range(steps + 1)]
                        + [2 * s + 2 * b - 1 for s in range(steps + 1)])
    q_frame = pos * per + jnp.arange(per, dtype=jnp.int32)
    q_clip = clip_of(q_frame, frames)[0]
    k_frame = ((pos - back_by)[:, None] * per
               + (jnp.arange(rows, dtype=jnp.int32) // FRAME)[None, :])
    k_clip = clip_of(k_frame.reshape(-1), frames)[0].reshape(k_frame.shape)
    kf, kc = k_frame[:, None, :], k_clip[:, None, :]
    qf, qc = q_frame[None, :, None], q_clip[None, :, None]
    mask = ((kf >= 0) & (kc == qc) & (kf <= qf) & (kf >= qf - (WIN - 1))).astype(jnp.float32)

    bf, f32 = jnp.bfloat16, jnp.float32
    width = heads * hs
    dma = pltpu.SemaphoreType.DMA
    out = pl.pallas_call(
        functools.partial(kernel, (n_out, reach, steps, q_cnt, heads, hs)),
        out_shape=jax.ShapeDtypeStruct((2, q_cnt, rows, dsl), bf),
        in_specs=[pl.BlockSpec(memory_space=pltpu.VMEM)] * 5,
        out_specs=pl.BlockSpec(memory_space=pltpu.VMEM),
        scratch_shapes=[
            pltpu.VMEM((steps, rows, width), bf),
            pltpu.VMEM((steps, rows, width), bf),
            pltpu.VMEM((steps + 1, rows, width), bf),
            pltpu.VMEM((steps + 1, rows, width), bf),
            pltpu.VMEM((n_out,) + out_weight.shape, bf),
            pltpu.VMEM((rows, width), f32),
            pltpu.VMEM((heads, rows, 1), f32),
            pltpu.VMEM((2 * rows, width), bf),
            pltpu.VMEM((2, q_cnt, 2 * rows, dsl), bf),
            pltpu.VMEM((2, q_cnt, 2 * rows, dsl), f32),
            pltpu.VMEM((2, q_cnt, 2 * rows, dsl), bf),
            pltpu.VMEM((2, q_cnt, rows, dsl), bf),
            pltpu.VMEM((2, q_cnt, rows, dsl), bf),
            pltpu.VMEM((q_cnt, rows, dsl), bf),
            pltpu.VMEM((q_cnt, rows, dsl), bf),
            dma((steps, 2)), dma((steps, 2)), dma((steps + 1, 2)), dma((steps + 1, 2)),
            dma((n_out - 1,)), dma((n_out - 1,)), dma((n_out - 1,)), dma((n_out - 1,)),
            dma, dma, dma((2,)), dma((2,)), dma((2,)), dma((2,)), dma, dma, dma,
        ],
        compiler_params=pltpu.CompilerParams(
            collective_id=0, has_side_effects=True, vmem_limit_bytes=56 * 1024 * 1024
        ),
    )(q_rot.reshape(rows, width), k_rot.reshape(rows, width), values, out_weight, mask)
    return jnp.transpose(out, (2, 1, 0, 3)).reshape(rows, 2 * q_cnt * dsl)


def solution(mesh):
    in_specs = (
        P("tm", "head"),
        P("tm", "head"),
        P("tm", "head"),
        P(),
        P(),
        P(),
        P(),
        P("head", "tm", None),
    )
    out_specs = P("tm", "head")
    return jax.shard_map(
        per_device, mesh=mesh, in_specs=in_specs, out_specs=out_specs, check_vma=False
    )
```

```python
import functools
import math

import jax
import jax.numpy as jnp
from jax import lax
from jax.experimental import pallas as pl
from jax.experimental.pallas import tpu as pltpu
from jax.sharding import PartitionSpec as P

GW = 16
WIN = 12
FRAME = 128
MESH = pl.DeviceIdType.MESH


def rope_freqs(width):
    steps = jnp.arange(width // 2, dtype=jnp.float32)
    return jnp.exp(steps * (-2.0 * math.log(10000.0) / width))


def clip_of(frame_global, frames):
    ends = jnp.cumsum(frames)
    starts = ends - frames
    inside = (
        (frame_global[:, None] >= starts[None, :]) & (frame_global[:, None] < ends[None, :])
    ).astype(jnp.int32)
    clip_id = jnp.sum(inside * jnp.arange(frames.shape[0], dtype=jnp.int32)[None, :], axis=1)
    return (clip_id, inside, starts)


def rotary(token_index, frames, frame_rate, head_size):
    frame_global = token_index // FRAME
    clip_id, inside, starts = clip_of(frame_global, frames)
    frame_start = jnp.sum(inside * starts[None, :], axis=1)
    rate_token = jnp.sum(inside * frame_rate[None, :], axis=1).astype(jnp.float32)
    in_frame = token_index % FRAME
    time_pos = (frame_global - frame_start).astype(jnp.float32) * 24.0 / rate_token
    row_pos = (in_frame // GW).astype(jnp.float32)
    col_pos = (in_frame % GW).astype(jnp.float32)
    side = head_size // 6 * 2
    depth = head_size - 2 * side
    angles = jnp.concatenate(
        [
            time_pos[:, None] * rope_freqs(depth)[None, :],
            row_pos[:, None] * rope_freqs(side)[None, :],
            col_pos[:, None] * rope_freqs(side)[None, :],
        ],
        axis=1,
    )
    return (jnp.cos(angles), jnp.sin(angles))


def norm_rotate(rows, gain, cosine, sine):
    values_f = rows.astype(jnp.float32)
    mean_sq = jnp.mean(values_f * values_f, axis=-1, keepdims=True)
    normed = values_f * lax.rsqrt(mean_sq + 1e-06) * gain
    half = rows.shape[-1] // 2
    first, second = (normed[..., :half], normed[..., half:])
    cos_b = cosine[:, None, :]
    sin_b = sine[:, None, :]
    return jnp.concatenate(
        [first * cos_b - second * sin_b, second * cos_b + first * sin_b], axis=-1
    ).astype(jnp.bfloat16)


def kernel(cfg, q_ref, k_ref, v_ref, w_ref, mask_ref, out_ref,
           qd, kb, vb, wg, num, den, ntx, nrx, dtx, drx, att, ptx, keep, rx1, stx, rx2, ytx, yrx,
           qd_s, qd_r, pt_s, pt_r, nu_s, nu_r, wu_s, wu_r, wd_s, wd_r, at_s, at_r,
           c_s, c_r, h_s, h_r, y_s, y_r, loc):
    n_out, reach, steps, q_cnt, heads, hs = cfg
    rows = q_ref.shape[0]
    pos = lax.axis_index("tm")
    head = lax.axis_index("head")
    o, b = pos // 2, pos % 2
    hi, lo = head // 2, head % 2
    partner = pos + 1 - 2 * b
    core = head + 1 - 2 * lo
    cross = lax.rem(head + 2, 4)
    has_up = o + 1 < n_out
    has_dn = o >= 1

    barrier = pltpu.get_barrier_semaphore()
    pl.semaphore_signal(barrier, inc=1, device_id={"tm": partner}, device_id_type=MESH)
    pl.semaphore_signal(barrier, inc=1, device_id={"head": core}, device_id_type=MESH)
    pl.semaphore_signal(barrier, inc=1, device_id={"head": cross}, device_id_type=MESH)

    @pl.when(has_up)
    def _():
        pl.semaphore_signal(barrier, inc=1, device_id={"tm": pos + 2}, device_id_type=MESH)

    @pl.when(has_dn)
    def _():
        pl.semaphore_signal(barrier, inc=1, device_id={"tm": pos - 2}, device_id_type=MESH)

    amount = 3 + has_up.astype(jnp.int32) + has_dn.astype(jnp.int32)
    pl.semaphore_wait(barrier, amount)

    def rcopy(src, dst, s, r, axis, index):
        return pltpu.make_async_remote_copy(
            src_ref=src, dst_ref=dst, send_sem=s, recv_sem=r,
            device_id={axis: index}, device_id_type=MESH)

    def q_at(s):
        return q_ref if s == 0 else qd.at[s - 1]

    def q_dn(s):
        return [rcopy(q_at(s - 1), q_at(s), qd_s.at[s - 1], qd_r.at[s - 1], "tm", pos - 2)]

    def n_up(s):
        return [rcopy(ntx.at[s - 1], nrx.at[s - 1], nu_s.at[s - 1, 0], nu_r.at[s - 1, 0],
                      "tm", pos + 2),
                rcopy(dtx.at[s - 1], drx.at[s - 1], nu_s.at[s - 1, 1], nu_r.at[s - 1, 1],
                      "tm", pos + 2)]

    pair_kv = [rcopy(k_ref, kb, pt_s.at[0], pt_r.at[0], "tm", partner),
               rcopy(v_ref, vb, pt_s.at[1], pt_r.at[1], "tm", partner)]

    def w_up(t):
        origin = jnp.maximum(o - t + 1, 0)
        return rcopy(wg.at[origin], wg.at[origin], wu_s.at[t - 1], wu_r.at[t - 1], "tm", pos + 2)

    def w_dn(t):
        origin = jnp.minimum(o + t - 1, n_out - 1)
        return rcopy(wg.at[origin], wg.at[origin], wd_s.at[t - 1], wd_r.at[t - 1], "tm", pos - 2)

    def start_all(cond, copies):
        @pl.when(cond)
        def _():
            for c in copies:
                c.start()

    def wait_recv(cond, copies):
        @pl.when(cond)
        def _():
            for c in copies:
                c.wait_recv()

    def wait_send(cond, copies):
        @pl.when(cond)
        def _():
            for c in copies:
                c.wait_send()

    def up_sends(t):
        return has_up & (o - t + 1 >= 0)

    def dn_sends(t):
        return has_dn & (o + t - 1 < n_out)

    def q_sends(s):
        return has_dn & (o + s - 1 < n_out)

    def n_sends(s):
        return has_up & (o + s < n_out)

    def n_gets(s):
        return has_dn & (o + s < n_out)

    scale = 1.0 / math.sqrt(hs)
    lane = lax.broadcasted_iota(jnp.int32, (rows, 128), 1)

    def attend(s, key_ref, value_ref, slot, first):
        query_ref = q_at(s)
        mask = jnp.concatenate(
            [jnp.broadcast_to(mask_ref[slot, f:f + 1, :], (FRAME, rows))
             for f in range(rows // FRAME)], axis=0)
        if first:
            den[s] = jnp.zeros((rows, 128), jnp.float32)

        def one(h, carry):
            at = pl.ds(pl.multiple_of(h * hs, hs), hs)
            scores = lax.dot_general(query_ref[:, at], key_ref[:, at], (((1,), (1,)), ((), ())),
                                     preferred_element_type=jnp.float32)
            probs = jnp.exp(scores * scale) * mask
            total = jnp.sum(probs, axis=1, keepdims=True)
            part = jnp.dot(probs.astype(jnp.bfloat16), value_ref[:, at],
                           preferred_element_type=jnp.float32)
            den[s] += jnp.where(lane == h, total, 0.0)
            if first:
                num[s, :, at] = part
            else:
                num[s, :, at] += part
            return carry

        lax.fori_loop(0, heads, one, 0)

    start_all(q_sends(1), q_dn(1))
    for c in pair_kv:
        c.start()
    own = pltpu.make_async_copy(w_ref, wg.at[o], loc)
    own.start()
    own.wait()
    start_all(up_sends(1), [w_up(1)])
    attend(0, k_ref, v_ref, 0, True)

    def down(t):
        wait_recv(o + t < n_out, [w_dn(t)])
        if t + 1 < n_out:
            start_all(dn_sends(t + 1), [w_dn(t + 1)])

    def up(t):
        wait_recv(o - t >= 0, [w_up(t)])
        if t + 1 < n_out:
            start_all(up_sends(t + 1), [w_up(t + 1)])

    for s in range(1, steps + 1):
        wait_recv(o + s < n_out, q_dn(s))
        if s < steps:
            start_all(q_sends(s + 1), q_dn(s + 1))
        if s == max(steps - 1, 1):
            start_all(dn_sends(1), [w_dn(1)])

        @pl.when(o + s < n_out)
        def _():
            attend(s, k_ref, v_ref, 2 * s, True)
        if s == 1:
            up(1)
    for c in pair_kv:
        c.wait_recv()

    def with_pair(s):
        cond = (o + s < n_out) & (((b == 0) & (s >= 1)) | ((b == 1) & (2 * s + 1 <= reach)))

        @pl.when(cond)
        def _():
            attend(s, kb, vb, 2 * s + 1, False)

    def add_up(s):
        if s < steps:
            @pl.when(n_gets(s))
            def _():
                for c in n_up(s + 1):
                    c.wait_recv()
                num[s] += nrx[s].astype(jnp.float32)
                wide = jnp.concatenate(
                    [drx[s], jnp.zeros((120, rows), jnp.float32)], axis=0)
                den[s] += jnp.transpose(wide)
        if s >= 1:
            @pl.when(n_sends(s))
            def _():
                ntx[s - 1] = num[s].astype(jnp.bfloat16)
                dtx[s - 1] = jnp.transpose(den[s])[0:8]
                for c in n_up(s):
                    c.start()

    with_pair(steps)
    add_up(steps)
    for s in range(steps - 1, -1, -1):
        with_pair(s)
    up(2)
    down(1)
    for s in range(steps - 1, -1, -1):
        add_up(s)

    for h in range(heads):
        at = slice(h * hs, (h + 1) * hs)
        att[0:rows, at] = (num[0, :, at] / den[0, :, h:h + 1]).astype(jnp.bfloat16)
    swap = rcopy(att.at[pl.ds(0, rows)], att.at[pl.ds(rows, rows)], at_s, at_r, "tm", partner)
    swap.start()
    for t in range(3, n_out):
        down(t - 1)
        up(t)
    down(n_out - 1)
    swap.wait_recv()

    def project(group, store):
        def one(k, carry):
            acc = None
            for h in range(heads):
                part = lax.dot_general(
                    att[:, h * hs:(h + 1) * hs], wg[group * q_cnt + k, h],
                    (((1,), (1,)), ((), ())), preferred_element_type=jnp.float32)
                acc = part if acc is None else acc + part
            store(k, acc)
            return carry
        if q_cnt == 1:
            one(0, 0)
        else:
            lax.fori_loop(0, q_cnt, one, 0)

    sides = (1 - hi, hi)
    c_copies = []
    for i, side in enumerate(sides):
        def put(k, acc, i=i):
            ptx[i, k] = acc.astype(jnp.bfloat16)
        project(2 * side + (1 - lo), put)
        copy = rcopy(ptx.at[i], rx1.at[i], c_s.at[i], c_r.at[i], "head", core)
        copy.start()
        c_copies.append(copy)
    for i, side in enumerate(sides):
        def put(k, acc, i=i):
            keep[i, k] = acc
        project(2 * side + lo, put)
    c_copies[0].wait_recv()
    h_copies = [None, None]
    for r in (1, 0):
        at = slice(r * rows, (r + 1) * rows)
        stx[r] = (keep[0, :, at] + rx1[0, :, at].astype(jnp.float32)).astype(jnp.bfloat16)
        h_copies[r] = rcopy(stx.at[r], rx2.at[r], h_s.at[r], h_r.at[r], "head", cross)
        h_copies[r].start()
    c_copies[1].wait_recv()

    def final(r):
        at = slice(r * rows, (r + 1) * rows)
        mine = keep[1, :, at] + rx1[1, :, at].astype(jnp.float32)
        return (mine + rx2[r].astype(jnp.float32)).astype(jnp.bfloat16)

    h_copies[1].wait_recv()
    ytx[...] = final(1)
    y_copy = rcopy(ytx, yrx, y_s, y_r, "tm", partner)
    y_copy.start()
    h_copies[0].wait_recv()
    if len(out_ref.shape) == 2:
        dsl = ytx.shape[-1]
        out_ref[:, pl.ds(pl.multiple_of(b * dsl, 128), dsl)] = final(0)[0]
        y_copy.wait_recv()
        out_ref[:, pl.ds(pl.multiple_of((1 - b) * dsl, 128), dsl)] = yrx[0]
    else:
        out_ref[b] = final(0)
        y_copy.wait_recv()
        out_ref[1 - b] = yrx[...]

    for c in pair_kv:
        c.wait_send()
    for s in range(1, steps + 1):
        wait_send(q_sends(s), q_dn(s))
        wait_send(n_sends(s), n_up(s))
    for t in range(1, n_out):
        wait_send(up_sends(t), [w_up(t)])
        wait_send(dn_sends(t), [w_dn(t)])
    for c in [swap, y_copy] + c_copies + h_copies:
        c.wait_send()


def per_device(queries, key_input, values, query_gain, key_gain, frames, frame_rate, out_weight):
    rows = queries.shape[0]
    hs = query_gain.shape[0]
    heads = queries.shape[1] // hs
    n = lax.axis_size("tm")
    m = lax.axis_size("head")
    n_out = n // 2
    per = rows // FRAME
    longest = n * per // 2
    back = min(WIN, longest) - 1
    reach = min((back + per - 1) // per, n - 1)
    steps = (reach + 1) // 2
    q_cnt = n_out // m
    dsl = out_weight.shape[1]

    pos = lax.axis_index("tm")
    b = pos % 2
    own_index = pos * rows + jnp.arange(rows, dtype=jnp.int32)
    cosine, sine = rotary(own_index, frames, frame_rate, hs)
    q_rot = norm_rotate(queries.reshape(rows, heads, hs), query_gain, cosine, sine)
    k_rot = norm_rotate(key_input.reshape(rows, heads, hs), key_gain, cosine, sine)

    frames_at = jnp.arange(per, dtype=jnp.int32)
    q_pos = jnp.stack([pos + 2 * (slot // 2) for slot in range(2 * steps + 2)])
    k_pos = jnp.stack([pos, pos + 1 - 2 * b] * (steps + 1))
    q_frame = q_pos[:, None] * per + frames_at[None, :]
    q_clip = clip_of(q_frame.reshape(-1), frames)[0].reshape(q_frame.shape)
    k_frame = (k_pos[:, None] * per
               + (jnp.arange(rows, dtype=jnp.int32) // FRAME)[None, :])
    k_clip = clip_of(k_frame.reshape(-1), frames)[0].reshape(k_frame.shape)
    kf, kc = k_frame[:, None, :], k_clip[:, None, :]
    qf, qc = q_frame[:, :, None], q_clip[:, :, None]
    mask = ((kc == qc) & (kf <= qf) & (kf >= qf - (WIN - 1))).astype(jnp.float32)

    bf, f32 = jnp.bfloat16, jnp.float32
    width = heads * hs
    flat = q_cnt == 1 and dsl % 128 == 0
    shape = (rows, 2 * dsl) if flat else (2, q_cnt, rows, dsl)
    dma = pltpu.SemaphoreType.DMA
    out = pl.pallas_call(
        functools.partial(kernel, (n_out, reach, steps, q_cnt, heads, hs)),
        out_shape=jax.ShapeDtypeStruct(shape, bf),
        in_specs=[pl.BlockSpec(memory_space=pltpu.VMEM)] * 5,
        out_specs=pl.BlockSpec(memory_space=pltpu.VMEM),
        scratch_shapes=[
            pltpu.VMEM((steps, rows, width), bf),
            pltpu.VMEM((rows, width), bf),
            pltpu.VMEM((rows, width), bf),
            pltpu.VMEM((n_out,) + out_weight.shape, bf),
            pltpu.VMEM((steps + 1, rows, width), f32),
            pltpu.VMEM((steps + 1, rows, 128), f32),
            pltpu.VMEM((steps, rows, width), bf),
            pltpu.VMEM((steps, rows, width), bf),
            pltpu.VMEM((steps, 8, rows), f32),
            pltpu.VMEM((steps, 8, rows), f32),
            pltpu.VMEM((2 * rows, width), bf),
            pltpu.VMEM((2, q_cnt, 2 * rows, dsl), bf),
            pltpu.VMEM((2, q_cnt, 2 * rows, dsl), f32),
            pltpu.VMEM((2, q_cnt, 2 * rows, dsl), bf),
            pltpu.VMEM((2, q_cnt, rows, dsl), bf),
            pltpu.VMEM((2, q_cnt, rows, dsl), bf),
            pltpu.VMEM((q_cnt, rows, dsl), bf),
            pltpu.VMEM((q_cnt, rows, dsl), bf),
            dma((steps,)), dma((steps,)), dma((2,)), dma((2,)), dma((steps, 2)), dma((steps, 2)),
            dma((n_out - 1,)), dma((n_out - 1,)), dma((n_out - 1,)), dma((n_out - 1,)),
            dma, dma, dma((2,)), dma((2,)), dma((2,)), dma((2,)), dma, dma, dma,
        ],
        compiler_params=pltpu.CompilerParams(
            collective_id=0, has_side_effects=True, vmem_limit_bytes=56 * 1024 * 1024
        ),
    )(q_rot.reshape(rows, width), k_rot.reshape(rows, width), values, out_weight, mask)
    if flat:
        return out
    return jnp.transpose(out, (2, 1, 0, 3)).reshape(rows, 2 * q_cnt * dsl)


def solution(mesh):
    in_specs = (
        P("tm", "head"),
        P("tm", "head"),
        P("tm", "head"),
        P(),
        P(),
        P(),
        P(),
        P("head", "tm", None),
    )
    out_specs = P("tm", "head")
    return jax.shard_map(
        per_device, mesh=mesh, in_specs=in_specs, out_specs=out_specs, check_vma=False
    )
```

```python
import functools
import math

import jax
import jax.numpy as jnp
from jax import lax
from jax.experimental import pallas as pl
from jax.experimental.pallas import tpu as pltpu
from jax.sharding import PartitionSpec as P

GW = 16
WIN = 12
FRAME = 128
MESH = pl.DeviceIdType.MESH


def rope_freqs(width):
    steps = jnp.arange(width // 2, dtype=jnp.float32)
    return jnp.exp(steps * (-2.0 * math.log(10000.0) / width))


def clip_of(frame_global, frames):
    ends = jnp.cumsum(frames)
    starts = ends - frames
    inside = (
        (frame_global[:, None] >= starts[None, :]) & (frame_global[:, None] < ends[None, :])
    ).astype(jnp.int32)
    clip_id = jnp.sum(inside * jnp.arange(frames.shape[0], dtype=jnp.int32)[None, :], axis=1)
    return (clip_id, inside, starts)


def rotary(token_index, frames, frame_rate, head_size):
    frame_global = token_index // FRAME
    clip_id, inside, starts = clip_of(frame_global, frames)
    frame_start = jnp.sum(inside * starts[None, :], axis=1)
    rate_token = jnp.sum(inside * frame_rate[None, :], axis=1).astype(jnp.float32)
    in_frame = token_index % FRAME
    time_pos = (frame_global - frame_start).astype(jnp.float32) * 24.0 / rate_token
    row_pos = (in_frame // GW).astype(jnp.float32)
    col_pos = (in_frame % GW).astype(jnp.float32)
    side = head_size // 6 * 2
    depth = head_size - 2 * side
    angles = jnp.concatenate(
        [
            time_pos[:, None] * rope_freqs(depth)[None, :],
            row_pos[:, None] * rope_freqs(side)[None, :],
            col_pos[:, None] * rope_freqs(side)[None, :],
        ],
        axis=1,
    )
    cosine, sine = jnp.cos(angles), jnp.sin(angles)
    return (jnp.concatenate([cosine, cosine], axis=1), jnp.concatenate([-sine, sine], axis=1))


def kernel(cfg, q_hbm, k_hbm, v_hbm, w_hbm, cos_ref, sin_ref, gain_ref, mask_ref, out_ref,
           q_ref, k_ref, v_ref, qd, kb, vb, wg, num, den, ntx, nrx, dtx, drx, att, ptx, keep, rx1, stx, rx2, ytx, yrx,
           qd_s, qd_r, pt_s, pt_r, nu_s, nu_r, wu_s, wu_r, wd_s, wd_r, at_s, at_r,
           c_s, c_r, h_s, h_r, y_s, y_r, loc):
    n_out, reach, steps, q_cnt, heads, hs = cfg
    rows = q_ref.shape[0]
    pos = lax.axis_index("tm")
    head = lax.axis_index("head")
    o, b = pos // 2, pos % 2
    hi, lo = head // 2, head % 2
    partner = pos + 1 - 2 * b
    core = head + 1 - 2 * lo
    cross = lax.rem(head + 2, 4)
    has_up = o + 1 < n_out
    has_dn = o >= 1

    loads = [pltpu.make_async_copy(src, dst, loc.at[i]) for i, (src, dst) in enumerate(
        [(w_hbm, wg.at[o]), (q_hbm, q_ref), (k_hbm, k_ref), (v_hbm, v_ref)])]
    for c in loads:
        c.start()

    barrier = pltpu.get_barrier_semaphore()
    pl.semaphore_signal(barrier, inc=1, device_id={"tm": partner}, device_id_type=MESH)
    pl.semaphore_signal(barrier, inc=1, device_id={"head": core}, device_id_type=MESH)
    pl.semaphore_signal(barrier, inc=1, device_id={"head": cross}, device_id_type=MESH)

    @pl.when(has_up)
    def _():
        pl.semaphore_signal(barrier, inc=1, device_id={"tm": pos + 2}, device_id_type=MESH)

    @pl.when(has_dn)
    def _():
        pl.semaphore_signal(barrier, inc=1, device_id={"tm": pos - 2}, device_id_type=MESH)

    amount = 3 + has_up.astype(jnp.int32) + has_dn.astype(jnp.int32)
    pl.semaphore_wait(barrier, amount)

    def rcopy(src, dst, s, r, axis, index):
        return pltpu.make_async_remote_copy(
            src_ref=src, dst_ref=dst, send_sem=s, recv_sem=r,
            device_id={axis: index}, device_id_type=MESH)

    def q_at(s):
        return q_ref if s == 0 else qd.at[s - 1]

    def q_dn(s):
        return [rcopy(q_at(s - 1), q_at(s), qd_s.at[s - 1], qd_r.at[s - 1], "tm", pos - 2)]

    def n_up(s):
        return [rcopy(ntx.at[s - 1], nrx.at[s - 1], nu_s.at[s - 1, 0], nu_r.at[s - 1, 0],
                      "tm", pos + 2),
                rcopy(dtx.at[s - 1], drx.at[s - 1], nu_s.at[s - 1, 1], nu_r.at[s - 1, 1],
                      "tm", pos + 2)]

    pair_kv = [rcopy(k_ref, kb, pt_s.at[0], pt_r.at[0], "tm", partner),
               rcopy(v_ref, vb, pt_s.at[1], pt_r.at[1], "tm", partner)]

    def w_up(t):
        origin = jnp.maximum(o - t + 1, 0)
        return rcopy(wg.at[origin], wg.at[origin], wu_s.at[t - 1], wu_r.at[t - 1], "tm", pos + 2)

    def w_dn(t):
        origin = jnp.minimum(o + t - 1, n_out - 1)
        return rcopy(wg.at[origin], wg.at[origin], wd_s.at[t - 1], wd_r.at[t - 1], "tm", pos - 2)

    def start_all(cond, copies):
        @pl.when(cond)
        def _():
            for c in copies:
                c.start()

    def wait_recv(cond, copies):
        @pl.when(cond)
        def _():
            for c in copies:
                c.wait_recv()

    def wait_send(cond, copies):
        @pl.when(cond)
        def _():
            for c in copies:
                c.wait_send()

    def up_sends(t):
        return has_up & (o - t + 1 >= 0)

    def dn_sends(t):
        return has_dn & (o + t - 1 < n_out)

    def q_sends(s):
        return has_dn & (o + s - 1 < n_out)

    def n_sends(s):
        return has_up & (o + s < n_out)

    def n_gets(s):
        return has_dn & (o + s < n_out)

    scale = 1.0 / math.sqrt(hs)
    lane = lax.broadcasted_iota(jnp.int32, (rows, 128), 1)

    def attend(s, key_ref, value_ref, slot, first):
        query_ref = q_at(s)
        mask = jnp.concatenate(
            [jnp.broadcast_to(mask_ref[slot, f:f + 1, :], (FRAME, rows))
             for f in range(rows // FRAME)], axis=0)
        if first:
            den[s] = jnp.zeros((rows, 128), jnp.float32)

        def one(h, carry):
            at = pl.ds(pl.multiple_of(h * hs, hs), hs)
            scores = lax.dot_general(query_ref[:, at], key_ref[:, at], (((1,), (1,)), ((), ())),
                                     preferred_element_type=jnp.float32)
            probs = jnp.exp(scores * scale) * mask
            total = jnp.sum(probs, axis=1, keepdims=True)
            part = jnp.dot(probs.astype(jnp.bfloat16), value_ref[:, at],
                           preferred_element_type=jnp.float32)
            den[s] += jnp.where(lane == h, total, 0.0)
            if first:
                num[s, :, at] = part
            else:
                num[s, :, at] += part
            return carry

        lax.fori_loop(0, heads, one, 0)

    def rotate(ref, row):
        gain = gain_ref[row:row + 1, :]
        for h in range(heads):
            at = slice(h * hs, (h + 1) * hs)
            x = ref[:, at].astype(jnp.float32)
            mean_sq = jnp.mean(x * x, axis=1, keepdims=True)
            x = x * lax.rsqrt(mean_sq + 1e-06) * gain
            ref[:, at] = (x * cos_ref[...]
                          + pltpu.roll(x, hs // 2, 1) * sin_ref[...]).astype(jnp.bfloat16)

    loads[0].wait()
    start_all(up_sends(1), [w_up(1)])
    loads[3].wait()
    pair_kv[1].start()
    loads[1].wait()
    rotate(q_ref, 0)
    start_all(q_sends(1), q_dn(1))
    loads[2].wait()
    rotate(k_ref, 1)
    pair_kv[0].start()
    attend(0, k_ref, v_ref, 0, True)

    def down(t):
        wait_recv(o + t < n_out, [w_dn(t)])
        if t + 1 < n_out:
            start_all(dn_sends(t + 1), [w_dn(t + 1)])

    def up(t):
        wait_recv(o - t >= 0, [w_up(t)])
        if t + 1 < n_out:
            start_all(up_sends(t + 1), [w_up(t + 1)])

    for s in range(1, steps + 1):
        wait_recv(o + s < n_out, q_dn(s))
        if s < steps:
            start_all(q_sends(s + 1), q_dn(s + 1))
        if s == max(steps - 1, 1):
            start_all(dn_sends(1), [w_dn(1)])

        @pl.when(o + s < n_out)
        def _():
            attend(s, k_ref, v_ref, 2 * s, True)
        if s == 1:
            up(1)
    for c in pair_kv:
        c.wait_recv()

    def with_pair(s):
        cond = (o + s < n_out) & (((b == 0) & (s >= 1)) | ((b == 1) & (2 * s + 1 <= reach)))

        @pl.when(cond)
        def _():
            attend(s, kb, vb, 2 * s + 1, False)

    def add_up(s):
        if s < steps:
            @pl.when(n_gets(s))
            def _():
                for c in n_up(s + 1):
                    c.wait_recv()
                num[s] += nrx[s].astype(jnp.float32)
                wide = jnp.concatenate(
                    [drx[s], jnp.zeros((120, rows), jnp.float32)], axis=0)
                den[s] += jnp.transpose(wide)
        if s >= 1:
            @pl.when(n_sends(s))
            def _():
                ntx[s - 1] = num[s].astype(jnp.bfloat16)
                dtx[s - 1] = jnp.transpose(den[s])[0:8]
                for c in n_up(s):
                    c.start()

    with_pair(steps)
    add_up(steps)
    for s in range(steps - 1, -1, -1):
        with_pair(s)
    up(2)
    down(1)
    for s in range(steps - 1, -1, -1):
        if s == 0:
            down(2)
        add_up(s)

    for h in range(heads):
        at = slice(h * hs, (h + 1) * hs)
        att[0:rows, at] = (num[0, :, at] / den[0, :, h:h + 1]).astype(jnp.bfloat16)
    swap = rcopy(att.at[pl.ds(0, rows)], att.at[pl.ds(rows, rows)], at_s, at_r, "tm", partner)
    swap.start()
    for t in range(3, n_out):
        down(t)
        up(t)
    swap.wait_recv()

    def project(group, store):
        def one(k, carry):
            acc = None
            for h in range(heads):
                part = lax.dot_general(
                    att[:, h * hs:(h + 1) * hs], wg[group * q_cnt + k, h],
                    (((1,), (1,)), ((), ())), preferred_element_type=jnp.float32)
                acc = part if acc is None else acc + part
            store(k, acc)
            return carry
        if q_cnt == 1:
            one(0, 0)
        else:
            lax.fori_loop(0, q_cnt, one, 0)

    sides = (1 - hi, hi)
    c_copies = []
    for i, side in enumerate(sides):
        def put(k, acc, i=i):
            ptx[i, k] = acc.astype(jnp.bfloat16)
        project(2 * side + (1 - lo), put)
        copy = rcopy(ptx.at[i], rx1.at[i], c_s.at[i], c_r.at[i], "head", core)
        copy.start()
        c_copies.append(copy)
    for i, side in enumerate(sides):
        def put(k, acc, i=i):
            keep[i, k] = acc
        project(2 * side + lo, put)
    c_copies[0].wait_recv()
    h_copies = [None, None]
    for r in (1, 0):
        at = slice(r * rows, (r + 1) * rows)
        stx[r] = (keep[0, :, at] + rx1[0, :, at].astype(jnp.float32)).astype(jnp.bfloat16)
        h_copies[r] = rcopy(stx.at[r], rx2.at[r], h_s.at[r], h_r.at[r], "head", cross)
        h_copies[r].start()
    c_copies[1].wait_recv()

    def final(r):
        at = slice(r * rows, (r + 1) * rows)
        mine = keep[1, :, at] + rx1[1, :, at].astype(jnp.float32)
        return (mine + rx2[r].astype(jnp.float32)).astype(jnp.bfloat16)

    h_copies[1].wait_recv()
    ytx[...] = final(1)
    y_copy = rcopy(ytx, yrx, y_s, y_r, "tm", partner)
    y_copy.start()
    h_copies[0].wait_recv()
    if len(out_ref.shape) == 2:
        dsl = ytx.shape[-1]
        out_ref[:, pl.ds(pl.multiple_of(b * dsl, 128), dsl)] = final(0)[0]
        y_copy.wait_recv()
        out_ref[:, pl.ds(pl.multiple_of((1 - b) * dsl, 128), dsl)] = yrx[0]
    else:
        out_ref[b] = final(0)
        y_copy.wait_recv()
        out_ref[1 - b] = yrx[...]

    for c in pair_kv:
        c.wait_send()
    for s in range(1, steps + 1):
        wait_send(q_sends(s), q_dn(s))
        wait_send(n_sends(s), n_up(s))
    for t in range(1, n_out):
        wait_send(up_sends(t), [w_up(t)])
        wait_send(dn_sends(t), [w_dn(t)])
    for c in [swap, y_copy] + c_copies + h_copies:
        c.wait_send()


def per_device(queries, key_input, values, query_gain, key_gain, frames, frame_rate, out_weight):
    rows = queries.shape[0]
    hs = query_gain.shape[0]
    heads = queries.shape[1] // hs
    n = lax.axis_size("tm")
    m = lax.axis_size("head")
    n_out = n // 2
    per = rows // FRAME
    longest = n * per // 2
    back = min(WIN, longest) - 1
    reach = min((back + per - 1) // per, n - 1)
    steps = (reach + 1) // 2
    q_cnt = n_out // m
    dsl = out_weight.shape[1]

    pos = lax.axis_index("tm")
    b = pos % 2
    own_index = pos * rows + jnp.arange(rows, dtype=jnp.int32)
    cosine, sine = rotary(own_index, frames, frame_rate, hs)
    gains = jnp.stack([query_gain, key_gain])

    frames_at = jnp.arange(per, dtype=jnp.int32)
    q_pos = jnp.stack([pos + 2 * (slot // 2) for slot in range(2 * steps + 2)])
    k_pos = jnp.stack([pos, pos + 1 - 2 * b] * (steps + 1))
    q_frame = q_pos[:, None] * per + frames_at[None, :]
    q_clip = clip_of(q_frame.reshape(-1), frames)[0].reshape(q_frame.shape)
    k_frame = (k_pos[:, None] * per
               + (jnp.arange(rows, dtype=jnp.int32) // FRAME)[None, :])
    k_clip = clip_of(k_frame.reshape(-1), frames)[0].reshape(k_frame.shape)
    kf, kc = k_frame[:, None, :], k_clip[:, None, :]
    qf, qc = q_frame[:, :, None], q_clip[:, :, None]
    mask = ((kc == qc) & (kf <= qf) & (kf >= qf - (WIN - 1))).astype(jnp.float32)

    bf, f32 = jnp.bfloat16, jnp.float32
    width = heads * hs
    flat = q_cnt == 1 and dsl % 128 == 0
    shape = (rows, 2 * dsl) if flat else (2, q_cnt, rows, dsl)
    dma = pltpu.SemaphoreType.DMA
    out = pl.pallas_call(
        functools.partial(kernel, (n_out, reach, steps, q_cnt, heads, hs)),
        out_shape=jax.ShapeDtypeStruct(shape, bf),
        in_specs=[pl.BlockSpec(memory_space=pl.ANY)] * 4
        + [pl.BlockSpec(memory_space=pltpu.VMEM)] * 4,
        out_specs=pl.BlockSpec(memory_space=pltpu.VMEM),
        scratch_shapes=[
            pltpu.VMEM((rows, width), bf),
            pltpu.VMEM((rows, width), bf),
            pltpu.VMEM((rows, width), bf),
            pltpu.VMEM((steps, rows, width), bf),
            pltpu.VMEM((rows, width), bf),
            pltpu.VMEM((rows, width), bf),
            pltpu.VMEM((n_out,) + out_weight.shape, bf),
            pltpu.VMEM((steps + 1, rows, width), f32),
            pltpu.VMEM((steps + 1, rows, 128), f32),
            pltpu.VMEM((steps, rows, width), bf),
            pltpu.VMEM((steps, rows, width), bf),
            pltpu.VMEM((steps, 8, rows), f32),
            pltpu.VMEM((steps, 8, rows), f32),
            pltpu.VMEM((2 * rows, width), bf),
            pltpu.VMEM((2, q_cnt, 2 * rows, dsl), bf),
            pltpu.VMEM((2, q_cnt, 2 * rows, dsl), f32),
            pltpu.VMEM((2, q_cnt, 2 * rows, dsl), bf),
            pltpu.VMEM((2, q_cnt, rows, dsl), bf),
            pltpu.VMEM((2, q_cnt, rows, dsl), bf),
            pltpu.VMEM((q_cnt, rows, dsl), bf),
            pltpu.VMEM((q_cnt, rows, dsl), bf),
            dma((steps,)), dma((steps,)), dma((2,)), dma((2,)), dma((steps, 2)), dma((steps, 2)),
            dma((n_out - 1,)), dma((n_out - 1,)), dma((n_out - 1,)), dma((n_out - 1,)),
            dma, dma, dma((2,)), dma((2,)), dma((2,)), dma((2,)), dma, dma, dma((4,)),
        ],
        compiler_params=pltpu.CompilerParams(
            collective_id=0, has_side_effects=True, vmem_limit_bytes=56 * 1024 * 1024
        ),
    )(queries, key_input, values, out_weight, cosine, sine, gains, mask)
    if flat:
        return out
    return jnp.transpose(out, (2, 1, 0, 3)).reshape(rows, 2 * q_cnt * dsl)


def solution(mesh):
    in_specs = (
        P("tm", "head"),
        P("tm", "head"),
        P("tm", "head"),
        P(),
        P(),
        P(),
        P(),
        P("head", "tm", None),
    )
    out_specs = P("tm", "head")
    return jax.shard_map(
        per_device, mesh=mesh, in_specs=in_specs, out_specs=out_specs, check_vma=False
    )
```

```python
import functools
import math

import jax
import jax.numpy as jnp
from jax import lax
from jax.experimental import pallas as pl
from jax.experimental.pallas import tpu as pltpu
from jax.sharding import PartitionSpec as P

GW = 16
WIN = 12
FRAME = 128
MESH = pl.DeviceIdType.MESH


def rope_freqs(width):
    steps = jnp.arange(width // 2, dtype=jnp.float32)
    return jnp.exp(steps * (-2.0 * math.log(10000.0) / width))


def clip_of(frame_global, frames):
    ends = jnp.cumsum(frames)
    starts = ends - frames
    inside = (
        (frame_global[:, None] >= starts[None, :]) & (frame_global[:, None] < ends[None, :])
    ).astype(jnp.int32)
    clip_id = jnp.sum(inside * jnp.arange(frames.shape[0], dtype=jnp.int32)[None, :], axis=1)
    return (clip_id, inside, starts)


def rotary(token_index, frames, frame_rate, head_size):
    frame_global = token_index // FRAME
    clip_id, inside, starts = clip_of(frame_global, frames)
    frame_start = jnp.sum(inside * starts[None, :], axis=1)
    rate_token = jnp.sum(inside * frame_rate[None, :], axis=1).astype(jnp.float32)
    in_frame = token_index % FRAME
    time_pos = (frame_global - frame_start).astype(jnp.float32) * 24.0 / rate_token
    row_pos = (in_frame // GW).astype(jnp.float32)
    col_pos = (in_frame % GW).astype(jnp.float32)
    side = head_size // 6 * 2
    depth = head_size - 2 * side
    angles = jnp.concatenate(
        [
            time_pos[:, None] * rope_freqs(depth)[None, :],
            row_pos[:, None] * rope_freqs(side)[None, :],
            col_pos[:, None] * rope_freqs(side)[None, :],
        ],
        axis=1,
    )
    cosine, sine = jnp.cos(angles), jnp.sin(angles)
    return (jnp.concatenate([cosine, cosine], axis=1), jnp.concatenate([-sine, sine], axis=1))


def kernel(cfg, q_hbm, k_hbm, v_hbm, w_hbm, cos_ref, sin_ref, gain_ref, mask_ref, out_ref,
           q_ref, k_ref, v_ref, qd, kb, vb, wg, num, den, ntx, nrx, dtx, drx, att, ptx, keep, rx1, stx, rx2, ytx, yrx,
           qd_s, qd_r, pt_s, pt_r, nu_s, nu_r, wu_s, wu_r, wd_s, wd_r, at_s, at_r,
           c_s, c_r, h_s, h_r, y_s, y_r, loc):
    n_out, reach, steps, q_cnt, heads, hs = cfg
    rows = q_ref.shape[0]
    pos = lax.axis_index("tm")
    head = lax.axis_index("head")
    o, b = pos // 2, pos % 2
    hi, lo = head // 2, head % 2
    partner = pos + 1 - 2 * b
    core = head + 1 - 2 * lo
    cross = lax.rem(head + 2, 4)
    has_up = o + 1 < n_out
    has_dn = o >= 1

    loads = [pltpu.make_async_copy(src, dst, loc.at[i]) for i, (src, dst) in enumerate(
        [(w_hbm, wg.at[o]), (q_hbm, q_ref), (k_hbm, k_ref), (v_hbm, v_ref)])]
    for c in loads:
        c.start()

    barrier = pltpu.get_barrier_semaphore()
    pl.semaphore_signal(barrier, inc=1, device_id={"tm": partner}, device_id_type=MESH)
    pl.semaphore_signal(barrier, inc=1, device_id={"head": core}, device_id_type=MESH)
    pl.semaphore_signal(barrier, inc=1, device_id={"head": cross}, device_id_type=MESH)

    @pl.when(has_up)
    def _():
        pl.semaphore_signal(barrier, inc=1, device_id={"tm": pos + 2}, device_id_type=MESH)

    @pl.when(has_dn)
    def _():
        pl.semaphore_signal(barrier, inc=1, device_id={"tm": pos - 2}, device_id_type=MESH)

    amount = 3 + has_up.astype(jnp.int32) + has_dn.astype(jnp.int32)
    pl.semaphore_wait(barrier, amount)

    def rcopy(src, dst, s, r, axis, index):
        return pltpu.make_async_remote_copy(
            src_ref=src, dst_ref=dst, send_sem=s, recv_sem=r,
            device_id={axis: index}, device_id_type=MESH)

    def q_at(s):
        return q_ref if s == 0 else qd.at[s - 1]

    def q_dn(s):
        return [rcopy(q_at(s - 1), q_at(s), qd_s.at[s - 1], qd_r.at[s - 1], "tm", pos - 2)]

    def n_up(s):
        return [rcopy(ntx.at[s - 1], nrx.at[s - 1], nu_s.at[s - 1, 0], nu_r.at[s - 1, 0],
                      "tm", pos + 2),
                rcopy(dtx.at[s - 1], drx.at[s - 1], nu_s.at[s - 1, 1], nu_r.at[s - 1, 1],
                      "tm", pos + 2)]

    pair_kv = [rcopy(k_ref, kb, pt_s.at[0], pt_r.at[0], "tm", partner),
               rcopy(v_ref, vb, pt_s.at[1], pt_r.at[1], "tm", partner)]

    def w_up(t):
        origin = jnp.maximum(o - t + 1, 0)
        return rcopy(wg.at[origin], wg.at[origin], wu_s.at[t - 1], wu_r.at[t - 1], "tm", pos + 2)

    def w_dn(t):
        origin = jnp.minimum(o + t - 1, n_out - 1)
        return rcopy(wg.at[origin], wg.at[origin], wd_s.at[t - 1], wd_r.at[t - 1], "tm", pos - 2)

    def start_all(cond, copies):
        @pl.when(cond)
        def _():
            for c in copies:
                c.start()

    def wait_recv(cond, copies):
        @pl.when(cond)
        def _():
            for c in copies:
                c.wait_recv()

    def wait_send(cond, copies):
        @pl.when(cond)
        def _():
            for c in copies:
                c.wait_send()

    def up_sends(t):
        return has_up & (o - t + 1 >= 0)

    def dn_sends(t):
        return has_dn & (o + t - 1 < n_out)

    def q_sends(s):
        return has_dn & (o + s - 1 < n_out)

    def n_sends(s):
        return has_up & (o + s < n_out)

    def n_gets(s):
        return has_dn & (o + s < n_out)

    scale = 1.0 / math.sqrt(hs)
    lane = lax.broadcasted_iota(jnp.int32, (rows, 128), 1)

    def attend(s, key_ref, value_ref, slot, first):
        query_ref = q_at(s)
        mask = jnp.concatenate(
            [jnp.broadcast_to(mask_ref[slot, f:f + 1, :], (FRAME, rows))
             for f in range(rows // FRAME)], axis=0)
        if first:
            den[s] = jnp.zeros((rows, 128), jnp.float32)

        def one(h, carry):
            at = pl.ds(pl.multiple_of(h * hs, hs), hs)
            scores = lax.dot_general(query_ref[:, at], key_ref[:, at], (((1,), (1,)), ((), ())),
                                     preferred_element_type=jnp.float32)
            probs = jnp.exp(scores * scale) * mask
            total = jnp.sum(probs, axis=1, keepdims=True)
            part = jnp.dot(probs.astype(jnp.bfloat16), value_ref[:, at],
                           preferred_element_type=jnp.float32)
            den[s] += jnp.where(lane == h, total, 0.0)
            if first:
                num[s, :, at] = part
            else:
                num[s, :, at] += part
            return carry

        lax.fori_loop(0, heads, one, 0)

    def rotate(ref, row):
        gain = gain_ref[row:row + 1, :]
        for h in range(heads):
            at = slice(h * hs, (h + 1) * hs)
            x = ref[:, at].astype(jnp.float32)
            mean_sq = jnp.mean(x * x, axis=1, keepdims=True)
            x = x * lax.rsqrt(mean_sq + 1e-06) * gain
            ref[:, at] = (x * cos_ref[...]
                          + pltpu.roll(x, hs // 2, 1) * sin_ref[...]).astype(jnp.bfloat16)

    loads[0].wait()
    start_all(up_sends(1), [w_up(1)])
    loads[3].wait()
    pair_kv[1].start()
    loads[1].wait()
    rotate(q_ref, 0)
    start_all(q_sends(1), q_dn(1))
    loads[2].wait()
    rotate(k_ref, 1)
    pair_kv[0].start()
    attend(0, k_ref, v_ref, 0, True)

    def down(t):
        wait_recv(o + t < n_out, [w_dn(t)])
        if t + 1 < n_out:
            start_all(dn_sends(t + 1), [w_dn(t + 1)])

    def up(t):
        wait_recv(o - t >= 0, [w_up(t)])
        if t + 1 < n_out:
            start_all(up_sends(t + 1), [w_up(t + 1)])

    for s in range(1, steps + 1):
        wait_recv(o + s < n_out, q_dn(s))
        if s < steps:
            start_all(q_sends(s + 1), q_dn(s + 1))
        if s == max(steps - 1, 1):
            start_all(dn_sends(1), [w_dn(1)])

        @pl.when(o + s < n_out)
        def _():
            attend(s, k_ref, v_ref, 2 * s, True)
        if s == 1:
            up(1)
    for c in pair_kv:
        c.wait_recv()

    def with_pair(s):
        cond = (o + s < n_out) & (((b == 0) & (s >= 1)) | ((b == 1) & (2 * s + 1 <= reach)))

        @pl.when(cond)
        def _():
            attend(s, kb, vb, 2 * s + 1, False)

    def add_up(s):
        if s < steps:
            @pl.when(n_gets(s))
            def _():
                for c in n_up(s + 1):
                    c.wait_recv()
                num[s] += nrx[s].astype(jnp.float32)
                wide = jnp.concatenate(
                    [drx[s], jnp.zeros((120, rows), jnp.float32)], axis=0)
                den[s] += jnp.transpose(wide)
        if s >= 1:
            @pl.when(n_sends(s))
            def _():
                ntx[s - 1] = num[s].astype(jnp.bfloat16)
                dtx[s - 1] = jnp.transpose(den[s])[0:8]
                for c in n_up(s):
                    c.start()

    with_pair(steps)
    add_up(steps)
    for s in range(steps - 1, -1, -1):
        with_pair(s)
    up(2)
    down(1)
    for s in range(steps - 1, -1, -1):
        if s == 0:
            down(2)
        add_up(s)

    for h in range(heads):
        at = slice(h * hs, (h + 1) * hs)
        att[0:rows, at] = (num[0, :, at] / den[0, :, h:h + 1]).astype(jnp.bfloat16)
    swap = rcopy(att.at[pl.ds(0, rows)], att.at[pl.ds(rows, rows)], at_s, at_r, "tm", partner)
    swap.start()
    last = n_out - 1
    for t in range(3, last if q_cnt == 1 else n_out):
        down(t)
        up(t)
    swap.wait_recv()

    def project(group, store):
        def one(k, carry):
            acc = None
            for h in range(heads):
                part = lax.dot_general(
                    att[:, h * hs:(h + 1) * hs], wg[group * q_cnt + k, h],
                    (((1,), (1,)), ((), ())), preferred_element_type=jnp.float32)
                acc = part if acc is None else acc + part
            store(k, acc)
            return carry
        if q_cnt == 1:
            one(0, 0)
        else:
            lax.fori_loop(0, q_cnt, one, 0)

    late = (o >= n_out // 2).astype(jnp.int32)
    group = [i + late * (3 - 2 * i) for i in range(4)]
    c_copies = [rcopy(ptx.at[p], rx1.at[p], c_s.at[p], c_r.at[p], "head", core) for p in range(2)]
    h_copies = [rcopy(stx.at[r], rx2.at[r], h_s.at[r], h_r.at[r], "head", cross)
                for r in range(2)]
    y_copy = rcopy(ytx, yrx, y_s, y_r, "tm", partner)
    mine = [(group[2 * p] // 2) == hi for p in range(2)]
    dsl = ytx.shape[-1]

    def partial(i):
        def put(k, acc):
            keep[i, k] = acc
        project(group[i], put)

        @pl.when(group[i] % 2 != lo)
        def _():
            ptx[i // 2] = keep[i].astype(jnp.bfloat16)
            c_copies[i // 2].start()

    def kept(p, at):
        i = 2 * p + lax.rem(lo + late, 2)
        return keep[i, :, at] + rx1[p, :, at].astype(jnp.float32)

    def give(p):
        c_copies[p].wait_recv()

        @pl.when(jnp.logical_not(mine[p]))
        def _():
            for r in (1, 0):
                stx[r] = kept(p, slice(r * rows, (r + 1) * rows)).astype(jnp.bfloat16)
                h_copies[r].start()

    def place(which, block):
        if len(out_ref.shape) == 2:
            out_ref[:, pl.ds(pl.multiple_of(which * dsl, 128), dsl)] = block[0]
        else:
            out_ref[which] = block

    def finish(p):
        @pl.when(mine[p])
        def _():
            for r in (1, 0):
                h_copies[r].wait_recv()
                total = (kept(p, slice(r * rows, (r + 1) * rows))
                         + rx2[r].astype(jnp.float32)).astype(jnp.bfloat16)
                if r == 1:
                    ytx[...] = total
                    y_copy.start()
                else:
                    place(b, total)

    partial(0)
    partial(1)
    partial(2)
    give(0)
    if q_cnt == 1:
        down(last)
        up(last)
    partial(3)
    finish(0)
    give(1)
    finish(1)
    y_copy.wait_recv()
    place(1 - b, yrx[...])

    for c in pair_kv:
        c.wait_send()
    for s in range(1, steps + 1):
        wait_send(q_sends(s), q_dn(s))
        wait_send(n_sends(s), n_up(s))
    for t in range(1, n_out):
        wait_send(up_sends(t), [w_up(t)])
        wait_send(dn_sends(t), [w_dn(t)])
    for c in [swap, y_copy] + c_copies + h_copies:
        c.wait_send()


def per_device(queries, key_input, values, query_gain, key_gain, frames, frame_rate, out_weight):
    rows = queries.shape[0]
    hs = query_gain.shape[0]
    heads = queries.shape[1] // hs
    n = lax.axis_size("tm")
    m = lax.axis_size("head")
    n_out = n // 2
    per = rows // FRAME
    longest = n * per // 2
    back = min(WIN, longest) - 1
    reach = min((back + per - 1) // per, n - 1)
    steps = (reach + 1) // 2
    q_cnt = n_out // m
    dsl = out_weight.shape[1]

    pos = lax.axis_index("tm")
    b = pos % 2
    own_index = pos * rows + jnp.arange(rows, dtype=jnp.int32)
    cosine, sine = rotary(own_index, frames, frame_rate, hs)
    gains = jnp.stack([query_gain, key_gain])

    frames_at = jnp.arange(per, dtype=jnp.int32)
    q_pos = jnp.stack([pos + 2 * (slot // 2) for slot in range(2 * steps + 2)])
    k_pos = jnp.stack([pos, pos + 1 - 2 * b] * (steps + 1))
    q_frame = q_pos[:, None] * per + frames_at[None, :]
    q_clip = clip_of(q_frame.reshape(-1), frames)[0].reshape(q_frame.shape)
    k_frame = (k_pos[:, None] * per
               + (jnp.arange(rows, dtype=jnp.int32) // FRAME)[None, :])
    k_clip = clip_of(k_frame.reshape(-1), frames)[0].reshape(k_frame.shape)
    kf, kc = k_frame[:, None, :], k_clip[:, None, :]
    qf, qc = q_frame[:, :, None], q_clip[:, :, None]
    mask = ((kc == qc) & (kf <= qf) & (kf >= qf - (WIN - 1))).astype(jnp.float32)

    bf, f32 = jnp.bfloat16, jnp.float32
    width = heads * hs
    flat = q_cnt == 1 and dsl % 128 == 0
    shape = (rows, 2 * dsl) if flat else (2, q_cnt, rows, dsl)
    dma = pltpu.SemaphoreType.DMA
    out = pl.pallas_call(
        functools.partial(kernel, (n_out, reach, steps, q_cnt, heads, hs)),
        out_shape=jax.ShapeDtypeStruct(shape, bf),
        in_specs=[pl.BlockSpec(memory_space=pl.ANY)] * 4
        + [pl.BlockSpec(memory_space=pltpu.VMEM)] * 4,
        out_specs=pl.BlockSpec(memory_space=pltpu.VMEM),
        scratch_shapes=[
            pltpu.VMEM((rows, width), bf),
            pltpu.VMEM((rows, width), bf),
            pltpu.VMEM((rows, width), bf),
            pltpu.VMEM((steps, rows, width), bf),
            pltpu.VMEM((rows, width), bf),
            pltpu.VMEM((rows, width), bf),
            pltpu.VMEM((n_out,) + out_weight.shape, bf),
            pltpu.VMEM((steps + 1, rows, width), f32),
            pltpu.VMEM((steps + 1, rows, 128), f32),
            pltpu.VMEM((steps, rows, width), bf),
            pltpu.VMEM((steps, rows, width), bf),
            pltpu.VMEM((steps, 8, rows), f32),
            pltpu.VMEM((steps, 8, rows), f32),
            pltpu.VMEM((2 * rows, width), bf),
            pltpu.VMEM((2, q_cnt, 2 * rows, dsl), bf),
            pltpu.VMEM((4, q_cnt, 2 * rows, dsl), f32),
            pltpu.VMEM((2, q_cnt, 2 * rows, dsl), bf),
            pltpu.VMEM((2, q_cnt, rows, dsl), bf),
            pltpu.VMEM((2, q_cnt, rows, dsl), bf),
            pltpu.VMEM((q_cnt, rows, dsl), bf),
            pltpu.VMEM((q_cnt, rows, dsl), bf),
            dma((steps,)), dma((steps,)), dma((2,)), dma((2,)), dma((steps, 2)), dma((steps, 2)),
            dma((n_out - 1,)), dma((n_out - 1,)), dma((n_out - 1,)), dma((n_out - 1,)),
            dma, dma, dma((2,)), dma((2,)), dma((2,)), dma((2,)), dma, dma, dma((4,)),
        ],
        compiler_params=pltpu.CompilerParams(
            collective_id=0, has_side_effects=True, vmem_limit_bytes=56 * 1024 * 1024
        ),
    )(queries, key_input, values, out_weight, cosine, sine, gains, mask)
    if flat:
        return out
    return jnp.transpose(out, (2, 1, 0, 3)).reshape(rows, 2 * q_cnt * dsl)


def solution(mesh):
    in_specs = (
        P("tm", "head"),
        P("tm", "head"),
        P("tm", "head"),
        P(),
        P(),
        P(),
        P(),
        P("head", "tm", None),
    )
    out_specs = P("tm", "head")
    return jax.shard_map(
        per_device, mesh=mesh, in_specs=in_specs, out_specs=out_specs, check_vma=False
    )
```

```python
import functools
import math

import jax
import jax.numpy as jnp
from jax import lax
from jax.experimental import pallas as pl
from jax.experimental.pallas import tpu as pltpu
from jax.sharding import PartitionSpec as P

GW = 16
WIN = 12
FRAME = 128
MESH = pl.DeviceIdType.MESH


def rope_freqs(width):
    steps = jnp.arange(width // 2, dtype=jnp.float32)
    return jnp.exp(steps * (-2.0 * math.log(10000.0) / width))


def clip_of(frame_global, frames):
    ends = jnp.cumsum(frames)
    starts = ends - frames
    inside = (
        (frame_global[:, None] >= starts[None, :]) & (frame_global[:, None] < ends[None, :])
    ).astype(jnp.int32)
    clip_id = jnp.sum(inside * jnp.arange(frames.shape[0], dtype=jnp.int32)[None, :], axis=1)
    return (clip_id, inside, starts)


def rotary(token_index, frames, frame_rate, head_size):
    frame_global = token_index // FRAME
    clip_id, inside, starts = clip_of(frame_global, frames)
    frame_start = jnp.sum(inside * starts[None, :], axis=1)
    rate_token = jnp.sum(inside * frame_rate[None, :], axis=1).astype(jnp.float32)
    in_frame = token_index % FRAME
    time_pos = (frame_global - frame_start).astype(jnp.float32) * 24.0 / rate_token
    row_pos = (in_frame // GW).astype(jnp.float32)
    col_pos = (in_frame % GW).astype(jnp.float32)
    side = head_size // 6 * 2
    depth = head_size - 2 * side
    angles = jnp.concatenate(
        [
            time_pos[:, None] * rope_freqs(depth)[None, :],
            row_pos[:, None] * rope_freqs(side)[None, :],
            col_pos[:, None] * rope_freqs(side)[None, :],
        ],
        axis=1,
    )
    cosine, sine = jnp.cos(angles), jnp.sin(angles)
    return (jnp.concatenate([cosine, cosine], axis=1), jnp.concatenate([-sine, sine], axis=1))


def kernel(cfg, q_hbm, k_hbm, v_hbm, w_hbm, cos_ref, sin_ref, gain_ref, mask_ref, out_ref,
           q_ref, k_ref, v_ref, qd, kb, vb, wg, num, den, ntx, nrx, dtx, drx, att, ptx, keep, rx1, stx, rx2, ytx, yrx,
           qd_s, qd_r, pt_s, pt_r, nu_s, nu_r, wu_s, wu_r, wd_s, wd_r, at_s, at_r,
           c_s, c_r, h_s, h_r, y_s, y_r, loc):
    n_out, reach, steps, q_cnt, heads, hs = cfg
    rows = q_ref.shape[0]
    pos = lax.axis_index("tm")
    head = lax.axis_index("head")
    o, b = pos // 2, pos % 2
    hi, lo = head // 2, head % 2
    partner = pos + 1 - 2 * b
    core = head + 1 - 2 * lo
    cross = lax.rem(head + 2, 4)
    has_up = o + 1 < n_out
    has_dn = o >= 1

    loads = [pltpu.make_async_copy(src, dst, loc.at[i]) for i, (src, dst) in enumerate(
        [(w_hbm, wg.at[o]), (q_hbm, q_ref), (k_hbm, k_ref), (v_hbm, v_ref)])]
    for c in loads:
        c.start()

    barrier = pltpu.get_barrier_semaphore()
    pl.semaphore_signal(barrier, inc=1, device_id={"tm": partner}, device_id_type=MESH)
    pl.semaphore_signal(barrier, inc=1, device_id={"head": core}, device_id_type=MESH)
    pl.semaphore_signal(barrier, inc=1, device_id={"head": cross}, device_id_type=MESH)

    @pl.when(has_up)
    def _():
        pl.semaphore_signal(barrier, inc=1, device_id={"tm": pos + 2}, device_id_type=MESH)

    @pl.when(has_dn)
    def _():
        pl.semaphore_signal(barrier, inc=1, device_id={"tm": pos - 2}, device_id_type=MESH)

    amount = 3 + has_up.astype(jnp.int32) + has_dn.astype(jnp.int32)
    pl.semaphore_wait(barrier, amount)

    def rcopy(src, dst, s, r, axis, index):
        return pltpu.make_async_remote_copy(
            src_ref=src, dst_ref=dst, send_sem=s, recv_sem=r,
            device_id={axis: index}, device_id_type=MESH)

    def q_at(s):
        return q_ref if s == 0 else qd.at[s - 1]

    def q_dn(s):
        return [rcopy(q_at(s - 1), q_at(s), qd_s.at[s - 1], qd_r.at[s - 1], "tm", pos - 2)]

    def n_up(s):
        return [rcopy(ntx.at[s - 1], nrx.at[s - 1], nu_s.at[s - 1, 0], nu_r.at[s - 1, 0],
                      "tm", pos + 2),
                rcopy(dtx.at[s - 1], drx.at[s - 1], nu_s.at[s - 1, 1], nu_r.at[s - 1, 1],
                      "tm", pos + 2)]

    pair_kv = [rcopy(k_ref, kb, pt_s.at[0], pt_r.at[0], "tm", partner),
               rcopy(v_ref, vb, pt_s.at[1], pt_r.at[1], "tm", partner)]

    def w_up(t):
        origin = jnp.maximum(o - t + 1, 0)
        return rcopy(wg.at[origin], wg.at[origin], wu_s.at[t - 1], wu_r.at[t - 1], "tm", pos + 2)

    def w_dn(t):
        origin = jnp.minimum(o + t - 1, n_out - 1)
        return rcopy(wg.at[origin], wg.at[origin], wd_s.at[t - 1], wd_r.at[t - 1], "tm", pos - 2)

    def start_all(cond, copies):
        @pl.when(cond)
        def _():
            for c in copies:
                c.start()

    def wait_recv(cond, copies):
        @pl.when(cond)
        def _():
            for c in copies:
                c.wait_recv()

    def wait_send(cond, copies):
        @pl.when(cond)
        def _():
            for c in copies:
                c.wait_send()

    def up_sends(t):
        return has_up & (o - t + 1 >= 0)

    def dn_sends(t):
        return has_dn & (o + t - 1 < n_out)

    def q_sends(s):
        return has_dn & (o + s - 1 < n_out)

    def n_sends(s):
        return has_up & (o + s < n_out)

    def n_gets(s):
        return has_dn & (o + s < n_out)

    scale = 1.0 / math.sqrt(hs)
    lane = lax.broadcasted_iota(jnp.int32, (rows, 128), 1)

    def attend(s, key_ref, value_ref, slot, first):
        query_ref = q_at(s)
        mask = jnp.concatenate(
            [jnp.broadcast_to(mask_ref[slot, f:f + 1, :], (FRAME, rows))
             for f in range(rows // FRAME)], axis=0)
        if first:
            den[s] = jnp.zeros((rows, 128), jnp.float32)

        def one(h, carry):
            at = pl.ds(pl.multiple_of(h * hs, hs), hs)
            scores = lax.dot_general(query_ref[:, at], key_ref[:, at], (((1,), (1,)), ((), ())),
                                     preferred_element_type=jnp.float32)
            probs = jnp.exp(scores * scale) * mask
            total = jnp.sum(probs, axis=1, keepdims=True)
            part = jnp.dot(probs.astype(jnp.bfloat16), value_ref[:, at],
                           preferred_element_type=jnp.float32)
            den[s] += jnp.where(lane == h, total, 0.0)
            if first:
                num[s, :, at] = part
            else:
                num[s, :, at] += part
            return carry

        lax.fori_loop(0, heads, one, 0, unroll=True)

    def rotate(ref, row):
        gain = gain_ref[row:row + 1, :]
        for h in range(heads):
            at = slice(h * hs, (h + 1) * hs)
            x = ref[:, at].astype(jnp.float32)
            mean_sq = jnp.mean(x * x, axis=1, keepdims=True)
            x = x * lax.rsqrt(mean_sq + 1e-06) * gain
            ref[:, at] = (x * cos_ref[...]
                          + pltpu.roll(x, hs // 2, 1) * sin_ref[...]).astype(jnp.bfloat16)

    loads[0].wait()
    start_all(up_sends(1), [w_up(1)])
    loads[3].wait()
    pair_kv[1].start()
    loads[1].wait()
    rotate(q_ref, 0)
    start_all(q_sends(1), q_dn(1))
    loads[2].wait()
    rotate(k_ref, 1)
    pair_kv[0].start()
    attend(0, k_ref, v_ref, 0, True)

    def down(t):
        wait_recv(o + t < n_out, [w_dn(t)])
        if t + 1 < n_out:
            start_all(dn_sends(t + 1), [w_dn(t + 1)])

    def up(t):
        wait_recv(o - t >= 0, [w_up(t)])
        if t + 1 < n_out:
            start_all(up_sends(t + 1), [w_up(t + 1)])

    for s in range(1, steps + 1):
        wait_recv(o + s < n_out, q_dn(s))
        if s < steps:
            start_all(q_sends(s + 1), q_dn(s + 1))
        if s == max(steps - 1, 1):
            start_all(dn_sends(1), [w_dn(1)])

        @pl.when(o + s < n_out)
        def _():
            attend(s, k_ref, v_ref, 2 * s, True)
        if s == 1:
            up(1)
    for c in pair_kv:
        c.wait_recv()

    def with_pair(s):
        cond = (o + s < n_out) & (((b == 0) & (s >= 1)) | ((b == 1) & (2 * s + 1 <= reach)))

        @pl.when(cond)
        def _():
            attend(s, kb, vb, 2 * s + 1, False)

    def add_up(s):
        if s < steps:
            @pl.when(n_gets(s))
            def _():
                for c in n_up(s + 1):
                    c.wait_recv()
                num[s] += nrx[s].astype(jnp.float32)
                wide = jnp.concatenate(
                    [drx[s], jnp.zeros((120, rows), jnp.float32)], axis=0)
                den[s] += jnp.transpose(wide)
        if s >= 1:
            @pl.when(n_sends(s))
            def _():
                ntx[s - 1] = num[s].astype(jnp.bfloat16)
                dtx[s - 1] = jnp.transpose(den[s])[0:8]
                for c in n_up(s):
                    c.start()

    with_pair(steps)
    add_up(steps)
    for s in range(steps - 1, -1, -1):
        with_pair(s)
    up(2)
    down(1)
    for s in range(steps - 1, -1, -1):
        if s == 0:
            down(2)
        add_up(s)

    for h in range(heads):
        at = slice(h * hs, (h + 1) * hs)
        att[0:rows, at] = (num[0, :, at] / den[0, :, h:h + 1]).astype(jnp.bfloat16)
    swap = rcopy(att.at[pl.ds(0, rows)], att.at[pl.ds(rows, rows)], at_s, at_r, "tm", partner)
    swap.start()
    for t in range(3, n_out):
        down(t)
        up(t)
    swap.wait_recv()

    def project(group, store):
        def one(k, carry):
            acc = None
            for h in range(heads):
                part = lax.dot_general(
                    att[:, h * hs:(h + 1) * hs], wg[group * q_cnt + k, h],
                    (((1,), (1,)), ((), ())), preferred_element_type=jnp.float32)
                acc = part if acc is None else acc + part
            store(k, acc)
            return carry
        if q_cnt == 1:
            one(0, 0)
        else:
            lax.fori_loop(0, q_cnt, one, 0)

    sides = (1 - hi, hi)
    c_copies = []
    for i, side in enumerate(sides):
        def put(k, acc, i=i):
            ptx[i, k] = acc.astype(jnp.bfloat16)
        project(2 * side + (1 - lo), put)
        copy = rcopy(ptx.at[i], rx1.at[i], c_s.at[i], c_r.at[i], "head", core)
        copy.start()
        c_copies.append(copy)
    for i, side in enumerate(sides):
        def put(k, acc, i=i):
            keep[i, k] = acc
        project(2 * side + lo, put)
    c_copies[0].wait_recv()
    h_copies = [None, None]
    for r in (1, 0):
        at = slice(r * rows, (r + 1) * rows)
        stx[r] = (keep[0, :, at] + rx1[0, :, at].astype(jnp.float32)).astype(jnp.bfloat16)
        h_copies[r] = rcopy(stx.at[r], rx2.at[r], h_s.at[r], h_r.at[r], "head", cross)
        h_copies[r].start()
    c_copies[1].wait_recv()

    def final(r):
        at = slice(r * rows, (r + 1) * rows)
        mine = keep[1, :, at] + rx1[1, :, at].astype(jnp.float32)
        return (mine + rx2[r].astype(jnp.float32)).astype(jnp.bfloat16)

    h_copies[1].wait_recv()
    ytx[...] = final(1)
    y_copy = rcopy(ytx, yrx, y_s, y_r, "tm", partner)
    y_copy.start()
    h_copies[0].wait_recv()
    if len(out_ref.shape) == 2:
        dsl = ytx.shape[-1]
        out_ref[:, pl.ds(pl.multiple_of(b * dsl, 128), dsl)] = final(0)[0]
        y_copy.wait_recv()
        out_ref[:, pl.ds(pl.multiple_of((1 - b) * dsl, 128), dsl)] = yrx[0]
    else:
        out_ref[b] = final(0)
        y_copy.wait_recv()
        out_ref[1 - b] = yrx[...]

    for c in pair_kv:
        c.wait_send()
    for s in range(1, steps + 1):
        wait_send(q_sends(s), q_dn(s))
        wait_send(n_sends(s), n_up(s))
    for t in range(1, n_out):
        wait_send(up_sends(t), [w_up(t)])
        wait_send(dn_sends(t), [w_dn(t)])
    for c in [swap, y_copy] + c_copies + h_copies:
        c.wait_send()


def per_device(queries, key_input, values, query_gain, key_gain, frames, frame_rate, out_weight):
    rows = queries.shape[0]
    hs = query_gain.shape[0]
    heads = queries.shape[1] // hs
    n = lax.axis_size("tm")
    m = lax.axis_size("head")
    n_out = n // 2
    per = rows // FRAME
    longest = n * per // 2
    back = min(WIN, longest) - 1
    reach = min((back + per - 1) // per, n - 1)
    steps = (reach + 1) // 2
    q_cnt = n_out // m
    dsl = out_weight.shape[1]

    pos = lax.axis_index("tm")
    b = pos % 2
    own_index = pos * rows + jnp.arange(rows, dtype=jnp.int32)
    cosine, sine = rotary(own_index, frames, frame_rate, hs)
    gains = jnp.stack([query_gain, key_gain])

    frames_at = jnp.arange(per, dtype=jnp.int32)
    q_pos = jnp.stack([pos + 2 * (slot // 2) for slot in range(2 * steps + 2)])
    k_pos = jnp.stack([pos, pos + 1 - 2 * b] * (steps + 1))
    q_frame = q_pos[:, None] * per + frames_at[None, :]
    q_clip = clip_of(q_frame.reshape(-1), frames)[0].reshape(q_frame.shape)
    k_frame = (k_pos[:, None] * per
               + (jnp.arange(rows, dtype=jnp.int32) // FRAME)[None, :])
    k_clip = clip_of(k_frame.reshape(-1), frames)[0].reshape(k_frame.shape)
    kf, kc = k_frame[:, None, :], k_clip[:, None, :]
    qf, qc = q_frame[:, :, None], q_clip[:, :, None]
    mask = ((kc == qc) & (kf <= qf) & (kf >= qf - (WIN - 1))).astype(jnp.float32)

    bf, f32 = jnp.bfloat16, jnp.float32
    width = heads * hs
    flat = q_cnt == 1 and dsl % 128 == 0
    shape = (rows, 2 * dsl) if flat else (2, q_cnt, rows, dsl)
    dma = pltpu.SemaphoreType.DMA
    out = pl.pallas_call(
        functools.partial(kernel, (n_out, reach, steps, q_cnt, heads, hs)),
        out_shape=jax.ShapeDtypeStruct(shape, bf),
        in_specs=[pl.BlockSpec(memory_space=pl.ANY)] * 4
        + [pl.BlockSpec(memory_space=pltpu.VMEM)] * 4,
        out_specs=pl.BlockSpec(memory_space=pltpu.VMEM),
        scratch_shapes=[
            pltpu.VMEM((rows, width), bf),
            pltpu.VMEM((rows, width), bf),
            pltpu.VMEM((rows, width), bf),
            pltpu.VMEM((steps, rows, width), bf),
            pltpu.VMEM((rows, width), bf),
            pltpu.VMEM((rows, width), bf),
            pltpu.VMEM((n_out,) + out_weight.shape, bf),
            pltpu.VMEM((steps + 1, rows, width), f32),
            pltpu.VMEM((steps + 1, rows, 128), f32),
            pltpu.VMEM((steps, rows, width), bf),
            pltpu.VMEM((steps, rows, width), bf),
            pltpu.VMEM((steps, 8, rows), f32),
            pltpu.VMEM((steps, 8, rows), f32),
            pltpu.VMEM((2 * rows, width), bf),
            pltpu.VMEM((2, q_cnt, 2 * rows, dsl), bf),
            pltpu.VMEM((2, q_cnt, 2 * rows, dsl), f32),
            pltpu.VMEM((2, q_cnt, 2 * rows, dsl), bf),
            pltpu.VMEM((2, q_cnt, rows, dsl), bf),
            pltpu.VMEM((2, q_cnt, rows, dsl), bf),
            pltpu.VMEM((q_cnt, rows, dsl), bf),
            pltpu.VMEM((q_cnt, rows, dsl), bf),
            dma((steps,)), dma((steps,)), dma((2,)), dma((2,)), dma((steps, 2)), dma((steps, 2)),
            dma((n_out - 1,)), dma((n_out - 1,)), dma((n_out - 1,)), dma((n_out - 1,)),
            dma, dma, dma((2,)), dma((2,)), dma((2,)), dma((2,)), dma, dma, dma((4,)),
        ],
        compiler_params=pltpu.CompilerParams(
            collective_id=0, has_side_effects=True, vmem_limit_bytes=56 * 1024 * 1024
        ),
    )(queries, key_input, values, out_weight, cosine, sine, gains, mask)
    if flat:
        return out
    return jnp.transpose(out, (2, 1, 0, 3)).reshape(rows, 2 * q_cnt * dsl)


def solution(mesh):
    in_specs = (
        P("tm", "head"),
        P("tm", "head"),
        P("tm", "head"),
        P(),
        P(),
        P(),
        P(),
        P("head", "tm", None),
    )
    out_specs = P("tm", "head")
    return jax.shard_map(
        per_device, mesh=mesh, in_specs=in_specs, out_specs=out_specs, check_vma=False
    )
```

```python
import functools
import math

import jax
import jax.numpy as jnp
from jax import lax
from jax.experimental import pallas as pl
from jax.experimental.pallas import tpu as pltpu
from jax.sharding import PartitionSpec as P

GW = 16
WIN = 12
FRAME = 128
MESH = pl.DeviceIdType.MESH


def rope_freqs(width):
    steps = jnp.arange(width // 2, dtype=jnp.float32)
    return jnp.exp(steps * (-2.0 * math.log(10000.0) / width))


def clip_of(frame_global, frames):
    ends = jnp.cumsum(frames)
    starts = ends - frames
    inside = (
        (frame_global[:, None] >= starts[None, :]) & (frame_global[:, None] < ends[None, :])
    ).astype(jnp.int32)
    clip_id = jnp.sum(inside * jnp.arange(frames.shape[0], dtype=jnp.int32)[None, :], axis=1)
    return (clip_id, inside, starts)


def rotary(token_index, frames, frame_rate, head_size):
    frame_global = token_index // FRAME
    clip_id, inside, starts = clip_of(frame_global, frames)
    frame_start = jnp.sum(inside * starts[None, :], axis=1)
    rate_token = jnp.sum(inside * frame_rate[None, :], axis=1).astype(jnp.float32)
    in_frame = token_index % FRAME
    time_pos = (frame_global - frame_start).astype(jnp.float32) * 24.0 / rate_token
    row_pos = (in_frame // GW).astype(jnp.float32)
    col_pos = (in_frame % GW).astype(jnp.float32)
    side = head_size // 6 * 2
    depth = head_size - 2 * side
    angles = jnp.concatenate(
        [
            time_pos[:, None] * rope_freqs(depth)[None, :],
            row_pos[:, None] * rope_freqs(side)[None, :],
            col_pos[:, None] * rope_freqs(side)[None, :],
        ],
        axis=1,
    )
    cosine, sine = jnp.cos(angles), jnp.sin(angles)
    return (jnp.concatenate([cosine, cosine], axis=1), jnp.concatenate([-sine, sine], axis=1))


def kernel(cfg, q_hbm, k_hbm, v_hbm, w_hbm, cos_ref, sin_ref, gain_ref, mask_ref, out_ref,
           q_ref, k_ref, v_ref, qd, kb, vb, wg, num, den, ntx, nrx, dtx, drx, att, ptx, keep, rx1, stx, rx2, ytx, yrx,
           qd_s, qd_r, pt_s, pt_r, nu_s, nu_r, wu_s, wu_r, wd_s, wd_r, at_s, at_r,
           c_s, c_r, h_s, h_r, y_s, y_r, loc):
    n_out, reach, steps, q_cnt, heads, hs = cfg
    rows = q_ref.shape[0]
    pos = lax.axis_index("tm")
    head = lax.axis_index("head")
    o, b = pos // 2, pos % 2
    hi, lo = head // 2, head % 2
    partner = pos + 1 - 2 * b
    core = head + 1 - 2 * lo
    cross = lax.rem(head + 2, 4)
    has_up = o + 1 < n_out
    has_dn = o >= 1

    loads = [pltpu.make_async_copy(src, dst, loc.at[i]) for i, (src, dst) in enumerate(
        [(w_hbm, wg.at[o]), (q_hbm, q_ref), (k_hbm, k_ref), (v_hbm, v_ref)])]
    for c in loads:
        c.start()

    barrier = pltpu.get_barrier_semaphore()
    pl.semaphore_signal(barrier, inc=1, device_id={"tm": partner}, device_id_type=MESH)
    pl.semaphore_signal(barrier, inc=1, device_id={"head": core}, device_id_type=MESH)
    pl.semaphore_signal(barrier, inc=1, device_id={"head": cross}, device_id_type=MESH)

    @pl.when(has_up)
    def _():
        pl.semaphore_signal(barrier, inc=1, device_id={"tm": pos + 2}, device_id_type=MESH)

    @pl.when(has_dn)
    def _():
        pl.semaphore_signal(barrier, inc=1, device_id={"tm": pos - 2}, device_id_type=MESH)

    amount = 3 + has_up.astype(jnp.int32) + has_dn.astype(jnp.int32)
    pl.semaphore_wait(barrier, amount)

    def rcopy(src, dst, s, r, axis, index):
        return pltpu.make_async_remote_copy(
            src_ref=src, dst_ref=dst, send_sem=s, recv_sem=r,
            device_id={axis: index}, device_id_type=MESH)

    def q_at(s):
        return q_ref if s == 0 else qd.at[s - 1]

    def q_dn(s):
        return [rcopy(q_at(s - 1), q_at(s), qd_s.at[s - 1], qd_r.at[s - 1], "tm", pos - 2)]

    def n_up(s):
        return [rcopy(ntx.at[s - 1], nrx.at[s - 1], nu_s.at[s - 1, 0], nu_r.at[s - 1, 0],
                      "tm", pos + 2),
                rcopy(dtx.at[s - 1], drx.at[s - 1], nu_s.at[s - 1, 1], nu_r.at[s - 1, 1],
                      "tm", pos + 2)]

    pair_kv = [rcopy(k_ref, kb, pt_s.at[0], pt_r.at[0], "tm", partner),
               rcopy(v_ref, vb, pt_s.at[1], pt_r.at[1], "tm", partner)]

    def w_up(t):
        origin = jnp.maximum(o - t + 1, 0)
        return rcopy(wg.at[origin], wg.at[origin], wu_s.at[t - 1], wu_r.at[t - 1], "tm", pos + 2)

    def w_dn(t):
        origin = jnp.minimum(o + t - 1, n_out - 1)
        return rcopy(wg.at[origin], wg.at[origin], wd_s.at[t - 1], wd_r.at[t - 1], "tm", pos - 2)

    def start_all(cond, copies):
        @pl.when(cond)
        def _():
            for c in copies:
                c.start()

    def wait_recv(cond, copies):
        @pl.when(cond)
        def _():
            for c in copies:
                c.wait_recv()

    def wait_send(cond, copies):
        @pl.when(cond)
        def _():
            for c in copies:
                c.wait_send()

    def up_sends(t):
        return has_up & (o - t + 1 >= 0)

    def dn_sends(t):
        return has_dn & (o + t - 1 < n_out)

    def q_sends(s):
        return has_dn & (o + s - 1 < n_out)

    def n_sends(s):
        return has_up & (o + s < n_out)

    def n_gets(s):
        return has_dn & (o + s < n_out)

    scale = 1.0 / math.sqrt(hs)
    lane = lax.broadcasted_iota(jnp.int32, (rows, 128), 1)

    def attend(s, key_ref, value_ref, slot, first):
        query_ref = q_at(s)
        mask = jnp.concatenate(
            [jnp.broadcast_to(mask_ref[slot, f:f + 1, :], (FRAME, rows))
             for f in range(rows // FRAME)], axis=0)
        if first:
            den[s] = jnp.zeros((rows, 128), jnp.float32)

        def one(h, carry):
            at = pl.ds(pl.multiple_of(h * hs, hs), hs)
            scores = lax.dot_general(query_ref[:, at], key_ref[:, at], (((1,), (1,)), ((), ())),
                                     preferred_element_type=jnp.float32)
            probs = jnp.exp(scores * scale) * mask
            total = jnp.sum(probs, axis=1, keepdims=True)
            part = jnp.dot(probs.astype(jnp.bfloat16), value_ref[:, at],
                           preferred_element_type=jnp.float32)
            den[s] += jnp.where(lane == h, total, 0.0)
            if first:
                num[s, :, at] = part
            else:
                num[s, :, at] += part
            return carry

        lax.fori_loop(0, heads, one, 0)

    def rotate(ref, row):
        gain = gain_ref[row:row + 1, :]
        for h in range(heads):
            at = slice(h * hs, (h + 1) * hs)
            x = ref[:, at].astype(jnp.float32)
            mean_sq = jnp.mean(x * x, axis=1, keepdims=True)
            x = x * lax.rsqrt(mean_sq + 1e-06) * gain
            ref[:, at] = (x * cos_ref[...]
                          + pltpu.roll(x, hs // 2, 1) * sin_ref[...]).astype(jnp.bfloat16)

    loads[0].wait()
    start_all(up_sends(1), [w_up(1)])
    loads[3].wait()
    pair_kv[1].start()
    loads[1].wait()
    rotate(q_ref, 0)
    start_all(q_sends(1), q_dn(1))
    loads[2].wait()
    rotate(k_ref, 1)
    pair_kv[0].start()
    attend(0, k_ref, v_ref, 0, True)

    def down(t):
        wait_recv(o + t < n_out, [w_dn(t)])
        if t + 1 < n_out:
            start_all(dn_sends(t + 1), [w_dn(t + 1)])

    def up(t):
        wait_recv(o - t >= 0, [w_up(t)])
        if t + 1 < n_out:
            start_all(up_sends(t + 1), [w_up(t + 1)])

    for s in range(1, steps + 1):
        wait_recv(o + s < n_out, q_dn(s))
        if s < steps:
            start_all(q_sends(s + 1), q_dn(s + 1))
        if s == max(steps - 1, 1):
            start_all(dn_sends(1), [w_dn(1)])

        @pl.when(o + s < n_out)
        def _():
            attend(s, k_ref, v_ref, 2 * s, True)
        if s == 1:
            up(1)
    for c in pair_kv:
        c.wait_recv()

    def with_pair(s):
        cond = (o + s < n_out) & (((b == 0) & (s >= 1)) | ((b == 1) & (2 * s + 1 <= reach)))

        @pl.when(cond)
        def _():
            attend(s, kb, vb, 2 * s + 1, False)

    def add_up(s):
        if s < steps:
            @pl.when(n_gets(s))
            def _():
                for c in n_up(s + 1):
                    c.wait_recv()
                num[s] += nrx[s].astype(jnp.float32)
                wide = jnp.concatenate(
                    [drx[s], jnp.zeros((120, rows), jnp.float32)], axis=0)
                den[s] += jnp.transpose(wide)
        if s >= 1:
            @pl.when(n_sends(s))
            def _():
                ntx[s - 1] = num[s].astype(jnp.bfloat16)
                dtx[s - 1] = jnp.transpose(den[s])[0:8]
                for c in n_up(s):
                    c.start()

    with_pair(steps)
    add_up(steps)
    for s in range(steps - 1, -1, -1):
        with_pair(s)
    up(2)
    down(1)
    for s in range(steps - 1, -1, -1):
        if s == 0:
            down(2)
        add_up(s)

    for h in range(heads):
        at = slice(h * hs, (h + 1) * hs)
        att[0:rows, at] = (num[0, :, at] / den[0, :, h:h + 1]).astype(jnp.bfloat16)
    swap = rcopy(att.at[pl.ds(0, rows)], att.at[pl.ds(rows, rows)], at_s, at_r, "tm", partner)
    swap.start()
    for t in range(3, n_out):
        down(t)
        up(t)
    swap.wait_recv()

    def project(group, store):
        def one(k, carry):
            weight = jnp.concatenate([wg[group * q_cnt + k, h] for h in range(heads)], axis=1)
            acc = lax.dot_general(att[...], weight, (((1,), (1,)), ((), ())),
                                  preferred_element_type=jnp.float32)
            store(k, acc)
            return carry
        if q_cnt == 1:
            one(0, 0)
        else:
            lax.fori_loop(0, q_cnt, one, 0)

    sides = (1 - hi, hi)
    c_copies = []
    for i, side in enumerate(sides):
        def put(k, acc, i=i):
            ptx[i, k] = acc.astype(jnp.bfloat16)
        project(2 * side + (1 - lo), put)
        copy = rcopy(ptx.at[i], rx1.at[i], c_s.at[i], c_r.at[i], "head", core)
        copy.start()
        c_copies.append(copy)
    for i, side in enumerate(sides):
        def put(k, acc, i=i):
            keep[i, k] = acc
        project(2 * side + lo, put)
    c_copies[0].wait_recv()
    h_copies = [None, None]
    for r in (1, 0):
        at = slice(r * rows, (r + 1) * rows)
        stx[r] = (keep[0, :, at] + rx1[0, :, at].astype(jnp.float32)).astype(jnp.bfloat16)
        h_copies[r] = rcopy(stx.at[r], rx2.at[r], h_s.at[r], h_r.at[r], "head", cross)
        h_copies[r].start()
    c_copies[1].wait_recv()

    def final(r):
        at = slice(r * rows, (r + 1) * rows)
        mine = keep[1, :, at] + rx1[1, :, at].astype(jnp.float32)
        return (mine + rx2[r].astype(jnp.float32)).astype(jnp.bfloat16)

    h_copies[1].wait_recv()
    ytx[...] = final(1)
    y_copy = rcopy(ytx, yrx, y_s, y_r, "tm", partner)
    y_copy.start()
    h_copies[0].wait_recv()
    if len(out_ref.shape) == 2:
        dsl = ytx.shape[-1]
        out_ref[:, pl.ds(pl.multiple_of(b * dsl, 128), dsl)] = final(0)[0]
        y_copy.wait_recv()
        out_ref[:, pl.ds(pl.multiple_of((1 - b) * dsl, 128), dsl)] = yrx[0]
    else:
        out_ref[b] = final(0)
        y_copy.wait_recv()
        out_ref[1 - b] = yrx[...]

    for c in pair_kv:
        c.wait_send()
    for s in range(1, steps + 1):
        wait_send(q_sends(s), q_dn(s))
        wait_send(n_sends(s), n_up(s))
    for t in range(1, n_out):
        wait_send(up_sends(t), [w_up(t)])
        wait_send(dn_sends(t), [w_dn(t)])
    for c in [swap, y_copy] + c_copies + h_copies:
        c.wait_send()


def per_device(queries, key_input, values, query_gain, key_gain, frames, frame_rate, out_weight):
    rows = queries.shape[0]
    hs = query_gain.shape[0]
    heads = queries.shape[1] // hs
    n = lax.axis_size("tm")
    m = lax.axis_size("head")
    n_out = n // 2
    per = rows // FRAME
    longest = n * per // 2
    back = min(WIN, longest) - 1
    reach = min((back + per - 1) // per, n - 1)
    steps = (reach + 1) // 2
    q_cnt = n_out // m
    dsl = out_weight.shape[1]

    pos = lax.axis_index("tm")
    b = pos % 2
    own_index = pos * rows + jnp.arange(rows, dtype=jnp.int32)
    cosine, sine = rotary(own_index, frames, frame_rate, hs)
    gains = jnp.stack([query_gain, key_gain])

    frames_at = jnp.arange(per, dtype=jnp.int32)
    q_pos = jnp.stack([pos + 2 * (slot // 2) for slot in range(2 * steps + 2)])
    k_pos = jnp.stack([pos, pos + 1 - 2 * b] * (steps + 1))
    q_frame = q_pos[:, None] * per + frames_at[None, :]
    q_clip = clip_of(q_frame.reshape(-1), frames)[0].reshape(q_frame.shape)
    k_frame = (k_pos[:, None] * per
               + (jnp.arange(rows, dtype=jnp.int32) // FRAME)[None, :])
    k_clip = clip_of(k_frame.reshape(-1), frames)[0].reshape(k_frame.shape)
    kf, kc = k_frame[:, None, :], k_clip[:, None, :]
    qf, qc = q_frame[:, :, None], q_clip[:, :, None]
    mask = ((kc == qc) & (kf <= qf) & (kf >= qf - (WIN - 1))).astype(jnp.float32)

    bf, f32 = jnp.bfloat16, jnp.float32
    width = heads * hs
    flat = q_cnt == 1 and dsl % 128 == 0
    shape = (rows, 2 * dsl) if flat else (2, q_cnt, rows, dsl)
    dma = pltpu.SemaphoreType.DMA
    out = pl.pallas_call(
        functools.partial(kernel, (n_out, reach, steps, q_cnt, heads, hs)),
        out_shape=jax.ShapeDtypeStruct(shape, bf),
        in_specs=[pl.BlockSpec(memory_space=pl.ANY)] * 4
        + [pl.BlockSpec(memory_space=pltpu.VMEM)] * 4,
        out_specs=pl.BlockSpec(memory_space=pltpu.VMEM),
        scratch_shapes=[
            pltpu.VMEM((rows, width), bf),
            pltpu.VMEM((rows, width), bf),
            pltpu.VMEM((rows, width), bf),
            pltpu.VMEM((steps, rows, width), bf),
            pltpu.VMEM((rows, width), bf),
            pltpu.VMEM((rows, width), bf),
            pltpu.VMEM((n_out,) + out_weight.shape, bf),
            pltpu.VMEM((steps + 1, rows, width), f32),
            pltpu.VMEM((steps + 1, rows, 128), f32),
            pltpu.VMEM((steps, rows, width), bf),
            pltpu.VMEM((steps, rows, width), bf),
            pltpu.VMEM((steps, 8, rows), f32),
            pltpu.VMEM((steps, 8, rows), f32),
            pltpu.VMEM((2 * rows, width), bf),
            pltpu.VMEM((2, q_cnt, 2 * rows, dsl), bf),
            pltpu.VMEM((2, q_cnt, 2 * rows, dsl), f32),
            pltpu.VMEM((2, q_cnt, 2 * rows, dsl), bf),
            pltpu.VMEM((2, q_cnt, rows, dsl), bf),
            pltpu.VMEM((2, q_cnt, rows, dsl), bf),
            pltpu.VMEM((q_cnt, rows, dsl), bf),
            pltpu.VMEM((q_cnt, rows, dsl), bf),
            dma((steps,)), dma((steps,)), dma((2,)), dma((2,)), dma((steps, 2)), dma((steps, 2)),
            dma((n_out - 1,)), dma((n_out - 1,)), dma((n_out - 1,)), dma((n_out - 1,)),
            dma, dma, dma((2,)), dma((2,)), dma((2,)), dma((2,)), dma, dma, dma((4,)),
        ],
        compiler_params=pltpu.CompilerParams(
            collective_id=0, has_side_effects=True, vmem_limit_bytes=56 * 1024 * 1024
        ),
    )(queries, key_input, values, out_weight, cosine, sine, gains, mask)
    if flat:
        return out
    return jnp.transpose(out, (2, 1, 0, 3)).reshape(rows, 2 * q_cnt * dsl)


def solution(mesh):
    in_specs = (
        P("tm", "head"),
        P("tm", "head"),
        P("tm", "head"),
        P(),
        P(),
        P(),
        P(),
        P("head", "tm", None),
    )
    out_specs = P("tm", "head")
    return jax.shard_map(
        per_device, mesh=mesh, in_specs=in_specs, out_specs=out_specs, check_vma=False
    )
```

```python
import functools
import math

import jax
import jax.numpy as jnp
from jax import lax
from jax.experimental import pallas as pl
from jax.experimental.pallas import tpu as pltpu
from jax.sharding import PartitionSpec as P

GW = 16
WIN = 12
FRAME = 128
MESH = pl.DeviceIdType.MESH


def rope_freqs(width):
    steps = jnp.arange(width // 2, dtype=jnp.float32)
    return jnp.exp(steps * (-2.0 * math.log(10000.0) / width))


def clip_of(frame_global, frames):
    ends = jnp.cumsum(frames)
    starts = ends - frames
    inside = (
        (frame_global[:, None] >= starts[None, :]) & (frame_global[:, None] < ends[None, :])
    ).astype(jnp.int32)
    clip_id = jnp.sum(inside * jnp.arange(frames.shape[0], dtype=jnp.int32)[None, :], axis=1)
    return (clip_id, inside, starts)


def rotary(token_index, frames, frame_rate, head_size):
    frame_global = token_index // FRAME
    clip_id, inside, starts = clip_of(frame_global, frames)
    frame_start = jnp.sum(inside * starts[None, :], axis=1)
    rate_token = jnp.sum(inside * frame_rate[None, :], axis=1).astype(jnp.float32)
    in_frame = token_index % FRAME
    time_pos = (frame_global - frame_start).astype(jnp.float32) * 24.0 / rate_token
    row_pos = (in_frame // GW).astype(jnp.float32)
    col_pos = (in_frame % GW).astype(jnp.float32)
    side = head_size // 6 * 2
    depth = head_size - 2 * side
    angles = jnp.concatenate(
        [
            time_pos[:, None] * rope_freqs(depth)[None, :],
            row_pos[:, None] * rope_freqs(side)[None, :],
            col_pos[:, None] * rope_freqs(side)[None, :],
        ],
        axis=1,
    )
    cosine, sine = jnp.cos(angles), jnp.sin(angles)
    return (jnp.concatenate([cosine, cosine], axis=1), jnp.concatenate([-sine, sine], axis=1))


def kernel(cfg, q_hbm, k_hbm, v_hbm, w_hbm, cos_ref, sin_ref, gain_ref, mask_ref, out_ref,
           q_ref, k_ref, v_ref, qd, kb, vb, wg, num, den, ntx, nrx, dtx, drx, att, ptx, keep, rx1, stx, rx2, ytx, yrx,
           qd_s, qd_r, pt_s, pt_r, nu_s, nu_r, wu_s, wu_r, wd_s, wd_r, at_s, at_r,
           c_s, c_r, h_s, h_r, y_s, y_r, loc):
    n_out, reach, steps, q_cnt, heads, hs = cfg
    rows = q_ref.shape[0]
    pos = lax.axis_index("tm")
    head = lax.axis_index("head")
    o, b = pos // 2, pos % 2
    hi, lo = head // 2, head % 2
    partner = pos + 1 - 2 * b
    core = head + 1 - 2 * lo
    cross = lax.rem(head + 2, 4)
    has_up = o + 1 < n_out
    has_dn = o >= 1

    loads = [pltpu.make_async_copy(src, dst, loc.at[i]) for i, (src, dst) in enumerate(
        [(w_hbm, wg.at[o]), (q_hbm, q_ref), (k_hbm, k_ref), (v_hbm, v_ref)])]
    for c in loads:
        c.start()

    barrier = pltpu.get_barrier_semaphore()
    pl.semaphore_signal(barrier, inc=1, device_id={"tm": partner}, device_id_type=MESH)
    pl.semaphore_signal(barrier, inc=1, device_id={"head": core}, device_id_type=MESH)
    pl.semaphore_signal(barrier, inc=1, device_id={"head": cross}, device_id_type=MESH)

    @pl.when(has_up)
    def _():
        pl.semaphore_signal(barrier, inc=1, device_id={"tm": pos + 2}, device_id_type=MESH)

    @pl.when(has_dn)
    def _():
        pl.semaphore_signal(barrier, inc=1, device_id={"tm": pos - 2}, device_id_type=MESH)

    amount = 3 + has_up.astype(jnp.int32) + has_dn.astype(jnp.int32)
    pl.semaphore_wait(barrier, amount)

    def rcopy(src, dst, s, r, axis, index):
        return pltpu.make_async_remote_copy(
            src_ref=src, dst_ref=dst, send_sem=s, recv_sem=r,
            device_id={axis: index}, device_id_type=MESH)

    def q_at(s):
        return q_ref if s == 0 else qd.at[s - 1]

    def q_dn(s):
        return [rcopy(q_at(s - 1), q_at(s), qd_s.at[s - 1], qd_r.at[s - 1], "tm", pos - 2)]

    def n_up(s):
        return [rcopy(ntx.at[s - 1], nrx.at[s - 1], nu_s.at[s - 1, 0], nu_r.at[s - 1, 0],
                      "tm", pos + 2),
                rcopy(dtx.at[s - 1], drx.at[s - 1], nu_s.at[s - 1, 1], nu_r.at[s - 1, 1],
                      "tm", pos + 2)]

    pair_kv = [rcopy(k_ref, kb, pt_s.at[0], pt_r.at[0], "tm", partner),
               rcopy(v_ref, vb, pt_s.at[1], pt_r.at[1], "tm", partner)]

    def w_up(t):
        origin = jnp.maximum(o - t + 1, 0)
        return rcopy(wg.at[origin], wg.at[origin], wu_s.at[t - 1], wu_r.at[t - 1], "tm", pos + 2)

    def w_dn(t):
        origin = jnp.minimum(o + t - 1, n_out - 1)
        return rcopy(wg.at[origin], wg.at[origin], wd_s.at[t - 1], wd_r.at[t - 1], "tm", pos - 2)

    def start_all(cond, copies):
        @pl.when(cond)
        def _():
            for c in copies:
                c.start()

    def wait_recv(cond, copies):
        @pl.when(cond)
        def _():
            for c in copies:
                c.wait_recv()

    def wait_send(cond, copies):
        @pl.when(cond)
        def _():
            for c in copies:
                c.wait_send()

    def up_sends(t):
        return has_up & (o - t + 1 >= 0)

    def dn_sends(t):
        return has_dn & (o + t - 1 < n_out)

    def q_sends(s):
        return has_dn & (o + s - 1 < n_out)

    def n_sends(s):
        return has_up & (o + s < n_out)

    def n_gets(s):
        return has_dn & (o + s < n_out)

    scale = 1.0 / math.sqrt(hs)
    lane = lax.broadcasted_iota(jnp.int32, (rows, 128), 1)

    def attend(s, key_ref, value_ref, slot, first):
        query_ref = q_at(s)
        mask = jnp.concatenate(
            [jnp.broadcast_to(mask_ref[slot, f:f + 1, :], (FRAME, rows))
             for f in range(rows // FRAME)], axis=0)
        if first:
            den[s] = jnp.zeros((rows, 128), jnp.float32)

        def one(h, carry):
            at = pl.ds(pl.multiple_of(h * hs, hs), hs)
            scores = lax.dot_general(query_ref[:, at], key_ref[:, at], (((1,), (1,)), ((), ())),
                                     preferred_element_type=jnp.float32)
            probs = jnp.exp(scores * scale) * mask
            total = jnp.sum(probs, axis=1, keepdims=True)
            part = jnp.dot(probs.astype(jnp.bfloat16), value_ref[:, at],
                           preferred_element_type=jnp.float32)
            den[s] += jnp.where(lane == h, total, 0.0)
            if first:
                num[s, :, at] = part
            else:
                num[s, :, at] += part
            return carry

        lax.fori_loop(0, heads, one, 0)

    def rotate(ref, row):
        gain = gain_ref[row:row + 1, :]
        for h in range(heads):
            at = slice(h * hs, (h + 1) * hs)
            x = ref[:, at].astype(jnp.float32)
            mean_sq = jnp.mean(x * x, axis=1, keepdims=True)
            x = x * lax.rsqrt(mean_sq + 1e-06) * gain
            ref[:, at] = (x * cos_ref[...]
                          + pltpu.roll(x, hs // 2, 1) * sin_ref[...]).astype(jnp.bfloat16)

    loads[0].wait()
    start_all(up_sends(1), [w_up(1)])
    loads[3].wait()
    pair_kv[1].start()
    loads[1].wait()
    rotate(q_ref, 0)
    start_all(q_sends(1), q_dn(1))
    start_all(dn_sends(1), [w_dn(1)])
    loads[2].wait()
    rotate(k_ref, 1)
    pair_kv[0].start()
    attend(0, k_ref, v_ref, 0, True)

    def down(t):
        wait_recv(o + t < n_out, [w_dn(t)])
        if t + 1 < n_out:
            start_all(dn_sends(t + 1), [w_dn(t + 1)])

    def up(t):
        wait_recv(o - t >= 0, [w_up(t)])
        if t + 1 < n_out:
            start_all(up_sends(t + 1), [w_up(t + 1)])

    for s in range(1, steps + 1):
        wait_recv(o + s < n_out, q_dn(s))
        if s < steps:
            start_all(q_sends(s + 1), q_dn(s + 1))

        @pl.when(o + s < n_out)
        def _():
            attend(s, k_ref, v_ref, 2 * s, True)
        if s == 1:
            up(1)
    for c in pair_kv:
        c.wait_recv()

    def with_pair(s):
        cond = (o + s < n_out) & (((b == 0) & (s >= 1)) | ((b == 1) & (2 * s + 1 <= reach)))

        @pl.when(cond)
        def _():
            attend(s, kb, vb, 2 * s + 1, False)

    def add_up(s):
        if s < steps:
            @pl.when(n_gets(s))
            def _():
                for c in n_up(s + 1):
                    c.wait_recv()
                num[s] += nrx[s].astype(jnp.float32)
                wide = jnp.concatenate(
                    [drx[s], jnp.zeros((120, rows), jnp.float32)], axis=0)
                den[s] += jnp.transpose(wide)
        if s >= 1:
            @pl.when(n_sends(s))
            def _():
                ntx[s - 1] = num[s].astype(jnp.bfloat16)
                dtx[s - 1] = jnp.transpose(den[s])[0:8]
                for c in n_up(s):
                    c.start()

    with_pair(steps)
    add_up(steps)
    for s in range(steps - 1, -1, -1):
        with_pair(s)
    up(2)
    down(1)
    for s in range(steps - 1, -1, -1):
        if s == 0:
            down(2)
        add_up(s)

    for h in range(heads):
        at = slice(h * hs, (h + 1) * hs)
        att[0:rows, at] = (num[0, :, at] / den[0, :, h:h + 1]).astype(jnp.bfloat16)
    swap = rcopy(att.at[pl.ds(0, rows)], att.at[pl.ds(rows, rows)], at_s, at_r, "tm", partner)
    swap.start()
    for t in range(3, n_out):
        down(t)
        up(t)
    swap.wait_recv()

    def project(group, store):
        def one(k, carry):
            weight = jnp.concatenate([wg[group * q_cnt + k, h] for h in range(heads)], axis=1)
            acc = lax.dot_general(att[...], weight, (((1,), (1,)), ((), ())),
                                  preferred_element_type=jnp.float32)
            store(k, acc)
            return carry
        if q_cnt == 1:
            one(0, 0)
        else:
            lax.fori_loop(0, q_cnt, one, 0)

    sides = (1 - hi, hi)
    c_copies = []
    for i, side in enumerate(sides):
        def put(k, acc, i=i):
            ptx[i, k] = acc.astype(jnp.bfloat16)
        project(2 * side + (1 - lo), put)
        copy = rcopy(ptx.at[i], rx1.at[i], c_s.at[i], c_r.at[i], "head", core)
        copy.start()
        c_copies.append(copy)
    for i, side in enumerate(sides):
        def put(k, acc, i=i):
            keep[i, k] = acc
        project(2 * side + lo, put)
    c_copies[0].wait_recv()
    h_copies = [None, None]
    for r in (1, 0):
        at = slice(r * rows, (r + 1) * rows)
        stx[r] = (keep[0, :, at] + rx1[0, :, at].astype(jnp.float32)).astype(jnp.bfloat16)
        h_copies[r] = rcopy(stx.at[r], rx2.at[r], h_s.at[r], h_r.at[r], "head", cross)
        h_copies[r].start()
    c_copies[1].wait_recv()

    def final(r):
        at = slice(r * rows, (r + 1) * rows)
        mine = keep[1, :, at] + rx1[1, :, at].astype(jnp.float32)
        return (mine + rx2[r].astype(jnp.float32)).astype(jnp.bfloat16)

    h_copies[1].wait_recv()
    ytx[...] = final(1)
    y_copy = rcopy(ytx, yrx, y_s, y_r, "tm", partner)
    y_copy.start()
    h_copies[0].wait_recv()
    if len(out_ref.shape) == 2:
        dsl = ytx.shape[-1]
        out_ref[:, pl.ds(pl.multiple_of(b * dsl, 128), dsl)] = final(0)[0]
        y_copy.wait_recv()
        out_ref[:, pl.ds(pl.multiple_of((1 - b) * dsl, 128), dsl)] = yrx[0]
    else:
        out_ref[b] = final(0)
        y_copy.wait_recv()
        out_ref[1 - b] = yrx[...]

    for c in pair_kv:
        c.wait_send()
    for s in range(1, steps + 1):
        wait_send(q_sends(s), q_dn(s))
        wait_send(n_sends(s), n_up(s))
    for t in range(1, n_out):
        wait_send(up_sends(t), [w_up(t)])
        wait_send(dn_sends(t), [w_dn(t)])
    for c in [swap, y_copy] + c_copies + h_copies:
        c.wait_send()


def per_device(queries, key_input, values, query_gain, key_gain, frames, frame_rate, out_weight):
    rows = queries.shape[0]
    hs = query_gain.shape[0]
    heads = queries.shape[1] // hs
    n = lax.axis_size("tm")
    m = lax.axis_size("head")
    n_out = n // 2
    per = rows // FRAME
    longest = n * per // 2
    back = min(WIN, longest) - 1
    reach = min((back + per - 1) // per, n - 1)
    steps = (reach + 1) // 2
    q_cnt = n_out // m
    dsl = out_weight.shape[1]

    pos = lax.axis_index("tm")
    b = pos % 2
    own_index = pos * rows + jnp.arange(rows, dtype=jnp.int32)
    cosine, sine = rotary(own_index, frames, frame_rate, hs)
    gains = jnp.stack([query_gain, key_gain])

    frames_at = jnp.arange(per, dtype=jnp.int32)
    q_pos = jnp.stack([pos + 2 * (slot // 2) for slot in range(2 * steps + 2)])
    k_pos = jnp.stack([pos, pos + 1 - 2 * b] * (steps + 1))
    q_frame = q_pos[:, None] * per + frames_at[None, :]
    q_clip = clip_of(q_frame.reshape(-1), frames)[0].reshape(q_frame.shape)
    k_frame = (k_pos[:, None] * per
               + (jnp.arange(rows, dtype=jnp.int32) // FRAME)[None, :])
    k_clip = clip_of(k_frame.reshape(-1), frames)[0].reshape(k_frame.shape)
    kf, kc = k_frame[:, None, :], k_clip[:, None, :]
    qf, qc = q_frame[:, :, None], q_clip[:, :, None]
    mask = ((kc == qc) & (kf <= qf) & (kf >= qf - (WIN - 1))).astype(jnp.float32)

    bf, f32 = jnp.bfloat16, jnp.float32
    width = heads * hs
    flat = q_cnt == 1 and dsl % 128 == 0
    shape = (rows, 2 * dsl) if flat else (2, q_cnt, rows, dsl)
    dma = pltpu.SemaphoreType.DMA
    out = pl.pallas_call(
        functools.partial(kernel, (n_out, reach, steps, q_cnt, heads, hs)),
        out_shape=jax.ShapeDtypeStruct(shape, bf),
        in_specs=[pl.BlockSpec(memory_space=pl.ANY)] * 4
        + [pl.BlockSpec(memory_space=pltpu.VMEM)] * 4,
        out_specs=pl.BlockSpec(memory_space=pltpu.VMEM),
        scratch_shapes=[
            pltpu.VMEM((rows, width), bf),
            pltpu.VMEM((rows, width), bf),
            pltpu.VMEM((rows, width), bf),
            pltpu.VMEM((steps, rows, width), bf),
            pltpu.VMEM((rows, width), bf),
            pltpu.VMEM((rows, width), bf),
            pltpu.VMEM((n_out,) + out_weight.shape, bf),
            pltpu.VMEM((steps + 1, rows, width), f32),
            pltpu.VMEM((steps + 1, rows, 128), f32),
            pltpu.VMEM((steps, rows, width), bf),
            pltpu.VMEM((steps, rows, width), bf),
            pltpu.VMEM((steps, 8, rows), f32),
            pltpu.VMEM((steps, 8, rows), f32),
            pltpu.VMEM((2 * rows, width), bf),
            pltpu.VMEM((2, q_cnt, 2 * rows, dsl), bf),
            pltpu.VMEM((2, q_cnt, 2 * rows, dsl), f32),
            pltpu.VMEM((2, q_cnt, 2 * rows, dsl), bf),
            pltpu.VMEM((2, q_cnt, rows, dsl), bf),
            pltpu.VMEM((2, q_cnt, rows, dsl), bf),
            pltpu.VMEM((q_cnt, rows, dsl), bf),
            pltpu.VMEM((q_cnt, rows, dsl), bf),
            dma((steps,)), dma((steps,)), dma((2,)), dma((2,)), dma((steps, 2)), dma((steps, 2)),
            dma((n_out - 1,)), dma((n_out - 1,)), dma((n_out - 1,)), dma((n_out - 1,)),
            dma, dma, dma((2,)), dma((2,)), dma((2,)), dma((2,)), dma, dma, dma((4,)),
        ],
        compiler_params=pltpu.CompilerParams(
            collective_id=0, has_side_effects=True, vmem_limit_bytes=56 * 1024 * 1024
        ),
    )(queries, key_input, values, out_weight, cosine, sine, gains, mask)
    if flat:
        return out
    return jnp.transpose(out, (2, 1, 0, 3)).reshape(rows, 2 * q_cnt * dsl)


def solution(mesh):
    in_specs = (
        P("tm", "head"),
        P("tm", "head"),
        P("tm", "head"),
        P(),
        P(),
        P(),
        P(),
        P("head", "tm", None),
    )
    out_specs = P("tm", "head")
    return jax.shard_map(
        per_device, mesh=mesh, in_specs=in_specs, out_specs=out_specs, check_vma=False
    )
```
